32 devices in a mesh: ctx: 8 (over y, x, core), head: 4 (over z).
Axes of the slice: x: 2, y: 2, z: 4, core: 2. Of those that a mesh axis runs over, the one named last changes fastest.
Arguments:
- block_order: int32 [16], replicated, may hold values from 0 to 15, as said below
- query_latent: bfloat16 [1024, 128, 576], P('ctx', 'head'), may hold values from -12 to 12
- key_latent: bfloat16 [1024, 576], P('ctx'), may hold values from -6 to 6
- normalizer: float32 [1024, 128], P('ctx', 'head'), may hold values from 6 to 9
- indexer_query: bfloat16 [1024, 64, 128], P('ctx', 'head'), may hold values from -8 to 8
- indexer_key: bfloat16 [1024, 128], P('ctx'), may hold values from -4 to 4
- indexer_weight: bfloat16 [1024, 64], P('ctx', 'head'), may hold values from -4 to 4
Outputs:
- query_grad: float32 [1024, 64, 128], P('ctx', 'head')
- key_grad: float32 [1024, 128], P(('ctx', 'head'))
The draws below stay inside these ranges and needn't reach their ends.
Inputs may be any that keep to these rules, and one draw needn't show every extreme that they name: `block_order`: entries 2 i and 2 i + 1 are the blocks stored on ctx index i; all entries together are each of 0 to 15 once, and the two entries of one index sum to 15.
All inputs are finite; a program needn't handle non-finite values.
Results may differ from the reference program's by a relative error of at most 0.0037.
Values may be sent and summed in bfloat16 or wider, within the bound.
A program may use at most 128 MiB of HBM per device.

```python
import math
import jax
import jax.numpy as jnp
from jax import lax

HEADS = 128
LATENT = 576
IDX_HEADS = 64
IDX_DIM = 128
HALF = 64
BLOCKS = 16
TOKENS = 1024


def scaled_rows(key, shape, lower, upper):
    return jnp.exp(jax.random.uniform(key, shape, jnp.float32, math.log(lower), math.log(upper)))


def draw_block_order(key, part):
    shuffled = jax.random.permutation(key, BLOCKS // 2).astype(jnp.int32)
    upper_block = BLOCKS - 1 - shuffled
    return jnp.stack((shuffled, upper_block), axis=1).reshape(-1).astype(jnp.int32)


def draw_query_latent(key, part):
    base_key = jax.random.fold_in(key, 21)
    scale_key = jax.random.fold_in(key, 22)
    row_scale = scaled_rows(scale_key, (TOKENS, HEADS, 1), 0.5, 4.0)
    values = jnp.clip(jax.random.normal(base_key, (TOKENS, HEADS, LATENT), jnp.float32), -3.0, 3.0)
    return (values * row_scale).astype(jnp.bfloat16)


def draw_key_latent(key, part):
    base_key = jax.random.fold_in(key, 23)
    scale_key = jax.random.fold_in(key, 24)
    row_scale = scaled_rows(scale_key, (TOKENS, 1), 0.5, 2.0)
    values = jnp.clip(jax.random.normal(base_key, (TOKENS, LATENT), jnp.float32), -3.0, 3.0)
    return (values * row_scale).astype(jnp.bfloat16)


def indexer_draw(key):
    query_key = jax.random.fold_in(key, 31)
    keyset_key = jax.random.fold_in(key, 32)
    weight_key = jax.random.fold_in(key, 33)
    query = jnp.clip(jax.random.normal(query_key, (TOKENS, IDX_HEADS, IDX_DIM), jnp.float32), -4.0, 4.0)
    keyset = jnp.clip(jax.random.normal(keyset_key, (TOKENS, IDX_DIM), jnp.float32), -4.0, 4.0)
    weight = jnp.clip(jax.random.normal(weight_key, (TOKENS, IDX_HEADS), jnp.float32), -4.0, 4.0)
    return (query, keyset, weight)


def draw_indexer_query(key, part):
    return indexer_draw(key)[0].astype(jnp.bfloat16)


def draw_indexer_key(key, part):
    return indexer_draw(key)[1].astype(jnp.bfloat16)


def draw_indexer_weight(key, part):
    return indexer_draw(key)[2].astype(jnp.bfloat16)


def shard_levels(stream_key, extent, split, least, top_value):
    def one(dim, shards_of):
        steps = jax.random.uniform(jax.random.fold_in(jax.random.fold_in(stream_key, 6), dim), (shards_of,), jnp.float32, least / len(split), top_value / len(split))
        return jnp.repeat(jnp.exp(steps), extent[dim] // shards_of).reshape((-1,) + (1,) * (len(extent) - dim - 1))

    factor_of = one(*split[0])
    for cut in split[1:]:
        factor_of = factor_of * one(*cut)
    return factor_of


def setup_inputs(seed: int = 0) -> dict:
    splits = jax.random.split(jax.random.key(seed), 8)
    block_order = draw_block_order(jax.random.fold_in(splits[7], 71), 0)
    query_latent = draw_query_latent(jax.random.fold_in(splits[7], 71), 0)
    key_latent = draw_key_latent(jax.random.fold_in(splits[7], 71), 0)
    normalizer = jnp.clip(6.0 + 3.0 * jax.random.uniform(splits[3], (TOKENS, HEADS), jnp.float32) ** shard_levels(splits[3], (TOKENS, HEADS), ((0, 8), (1, 4)), -0.2, 0.2), 6.0, 9.0)
    indexer_query = draw_indexer_query(jax.random.fold_in(splits[7], 71), 0)
    indexer_key = draw_indexer_key(jax.random.fold_in(splits[7], 71), 0)
    indexer_weight = draw_indexer_weight(jax.random.fold_in(splits[7], 71), 0)
    return {"block_order": block_order, "query_latent": query_latent, "key_latent": key_latent, "normalizer": normalizer, "indexer_query": indexer_query, "indexer_key": indexer_key, "indexer_weight": indexer_weight}


mla_scale = 192.0 ** -0.5
loss_scale = 64.0


def reference(block_order, query_latent, key_latent, normalizer, indexer_query, indexer_key, indexer_weight):
    query_rows = 2 * HALF
    block_count = TOKENS // query_rows
    positions = (block_order[:, None] * HALF + jnp.arange(HALF, dtype=jnp.int32)[None, :]).reshape(-1).astype(jnp.int32)
    kv_float = key_latent.astype(jnp.float32)
    key_float = indexer_key.astype(jnp.float32)
    idx_scale = (IDX_HEADS * IDX_DIM) ** -0.5

    def scan_step(key_accum, pieces):
        query_block, lse_block, idx_block, weight_block, query_pos = pieces
        scores = jnp.einsum('thl,sl->ths', query_block.astype(jnp.float32), kv_float) * mla_scale
        visible = positions[None, :] <= query_pos[:, None]
        target_sum = jnp.where(visible, jnp.sum(jnp.exp(scores - lse_block[:, :, None]), axis=1), 0.0)
        row_total = jnp.sum(target_sum, axis=1, keepdims=True)
        idx_dot = jnp.einsum('tjd,sd->tjs', idx_block.astype(jnp.float32), key_float)
        logits = idx_scale * jnp.sum(weight_block.astype(jnp.float32)[:, :, None] * jnp.maximum(idx_dot, 0.0), axis=1)
        row_top = jnp.max(jnp.where(visible, logits, -jnp.inf), axis=1, keepdims=True)
        exp_logit = jnp.where(visible, jnp.exp(logits - row_top), 0.0)
        norm_sum = jnp.sum(exp_logit, axis=1, keepdims=True)
        grad_logit = jnp.where(visible, loss_scale * (exp_logit / norm_sum - target_sum / row_total), 0.0).astype(jnp.bfloat16)
        weight_scaled = weight_block.astype(jnp.float32) * idx_scale
        coefficient = jnp.where(idx_dot > 0, grad_logit.astype(jnp.float32)[:, None, :] * weight_scaled[:, :, None], 0.0).astype(jnp.bfloat16)
        coeff_float = coefficient.astype(jnp.float32)
        query_part = jnp.einsum('tjs,sd->tjd', coeff_float, key_float)
        key_accum = key_accum + jnp.einsum('tjs,tjd->sd', coeff_float, idx_block.astype(jnp.float32))
        return key_accum, query_part

    pieces = (
        query_latent.reshape(block_count, query_rows, HEADS, LATENT),
        normalizer.reshape(block_count, query_rows, HEADS),
        indexer_query.reshape(block_count, query_rows, IDX_HEADS, IDX_DIM),
        indexer_weight.reshape(block_count, query_rows, IDX_HEADS),
        positions.reshape(block_count, query_rows),
    )
    key_grad, query_parts = lax.scan(scan_step, jnp.zeros((TOKENS, IDX_DIM), jnp.float32), pieces)
    query_grad = query_parts.reshape(TOKENS, IDX_HEADS, IDX_DIM)
    return query_grad, key_grad
```

```python
import functools
import math

import jax
import jax.numpy as jnp
from jax import lax
from jax.experimental import pallas as pl
from jax.experimental.pallas import tpu as pltpu
from jax.sharding import PartitionSpec as P

MESH = pl.DeviceIdType.MESH
mla_scale = 192.0 ** (-0.5)
loss_scale = 64.0
log2e = math.log2(math.e)
NT_DIMS = (((1,), (1,)), ((), ()))
TN_DIMS = (((0,), (0,)), ((), ()))


def enter(groups, shares):
    ctx, head = lax.axis_index("ctx"), lax.axis_index("head")
    group, core = ctx // 2, lax.rem(ctx, 2)
    barrier = pltpu.get_barrier_semaphore()
    count = 0
    if groups:
        for step in range(1, groups):
            peer = lax.rem(group + step, groups) * 2 + core
            pl.semaphore_signal(barrier, 1, device_id={"ctx": peer}, device_id_type=MESH)
        pl.semaphore_signal(
            barrier, 1, device_id={"ctx": group * 2 + 1 - core}, device_id_type=MESH
        )
        count += groups
    for step in range(1, shares):
        peer = lax.rem(head + step, shares)
        pl.semaphore_signal(barrier, 1, device_id={"head": peer}, device_id_type=MESH)
    count += shares - 1
    pl.semaphore_wait(barrier, count)


def remote(src, dst, send, recv, device):
    return pltpu.make_async_remote_copy(
        src_ref=src, dst_ref=dst, send_sem=send, recv_sem=recv, device_id=device, device_id_type=MESH
    )


def gather_kernel(
    groups, shares, lat, idx, iq, iw, all_lat, all_idx, iq_recv, iw_recv,
    local, qs, qr, ws, wr, ds, dr, fs, fr,
):
    ctx, head = lax.axis_index("ctx"), lax.axis_index("head")
    group, core = ctx // 2, lax.rem(ctx, 2)
    sibling = group * 2 + 1 - core
    rows = lat.shape[0]
    half = rows // 2
    share = half // shares
    own = [
        pltpu.make_async_copy(lat, all_lat.at[ctx], local.at[0]),
        pltpu.make_async_copy(idx, all_idx.at[ctx], local.at[1]),
    ]
    for e in range(2):
        take = pl.ds(pl.multiple_of(e * half + head * share, share), share)
        own.append(pltpu.make_async_copy(iq.at[take], iq_recv.at[head, e], local.at[2 + e]))
        own.append(pltpu.make_async_copy(iw.at[take], iw_recv.at[head, e], local.at[4 + e]))
    for copy in own:
        copy.start()
    enter(groups, shares)
    sent = []
    for step in range(1, groups):
        peer = lax.rem(group + step, groups) * 2 + core
        for k, (src, dst) in enumerate(((lat, all_lat), (idx, all_idx))):
            copy = remote(src, dst.at[ctx], ds.at[k, step], dr.at[k, step], {"ctx": peer})
            copy.start()
            sent.append(copy)
    for k, (src, dst) in enumerate(((lat, all_lat), (idx, all_idx))):
        copy = remote(src, dst.at[ctx], fs.at[k, 0], fr.at[k, 0], {"ctx": sibling})
        copy.start()
        sent.append(copy)
    for step in range(1, shares):
        peer = lax.rem(head + step, shares)
        for e in range(2):
            take = pl.ds(pl.multiple_of(e * half + peer * share, share), share)
            for src, dst, s, r in ((iq, iq_recv, qs, qr), (iw, iw_recv, ws, wr)):
                copy = remote(
                    src.at[take], dst.at[head, e], s.at[step, e], r.at[step, e], {"head": peer}
                )
                copy.start()
                sent.append(copy)
    for step in range(1, groups):
        source = lax.rem(group + groups - step, groups) * 2 + core
        for k, dst in enumerate((all_lat, all_idx)):
            slot = dst.at[source]
            remote(slot, slot, ds.at[k, step], dr.at[k, step], {"ctx": sibling}).wait_recv()
            copy = remote(slot, slot, fs.at[k, step], fr.at[k, step], {"ctx": sibling})
            copy.start()
            sent.append(copy)
    for step in range(groups):
        source = lax.rem(group + groups - step, groups) * 2 + 1 - core
        for k, dst in enumerate((all_lat, all_idx)):
            slot = dst.at[source]
            remote(slot, slot, fs.at[k, step], fr.at[k, step], {"ctx": sibling}).wait_recv()
    for step in range(1, shares):
        source = lax.rem(head + shares - step, shares)
        for e in range(2):
            for dst, s, r in ((iq_recv, qs, qr), (iw_recv, ws, wr)):
                slot = dst.at[source, e]
                remote(slot, slot, s.at[step, e], r.at[step, e], {"head": source}).wait_recv()
    for copy in sent:
        copy.wait_send()
    for copy in own:
        copy.wait()


def gather(lat, idx, iq, iw, cycle, shares):
    groups = cycle // 2
    rows = lat.shape[0]
    share = rows // 2 // shares
    dma = pltpu.SemaphoreType.DMA
    return pl.pallas_call(
        functools.partial(gather_kernel, groups, shares),
        out_shape=(
            jax.ShapeDtypeStruct((cycle,) + lat.shape, lat.dtype),
            jax.ShapeDtypeStruct((cycle,) + idx.shape, idx.dtype),
            jax.ShapeDtypeStruct((shares, 2, share) + iq.shape[1:], iq.dtype),
            jax.ShapeDtypeStruct((shares, 2, share) + iw.shape[1:], iw.dtype),
        ),
        in_specs=[pl.BlockSpec(memory_space=pl.ANY)] * 4,
        out_specs=[pl.BlockSpec(memory_space=pltpu.VMEM)] * 4,
        scratch_shapes=[
            dma((6,)),
            dma((shares, 2)), dma((shares, 2)), dma((shares, 2)), dma((shares, 2)),
            dma((2, groups)), dma((2, groups)), dma((2, groups)), dma((2, groups)),
        ],
        compiler_params=pltpu.CompilerParams(collective_id=0, has_side_effects=True),
        name="gather",
    )(lat, idx, iq, iw)


def forward_kernel(
    shares, tile, order, q, norm, lat, idx, iq, iw, sums, probs, idx_sorted, lat_sorted, logits
):
    step, steps = pl.program_id(0), pl.num_programs(0)
    ctx, head = lax.axis_index("ctx"), lax.axis_index("head")
    blocks = order.shape[0]
    half = lat.shape[0] // blocks
    tokens = lat.shape[0]
    tiles = tokens // tile
    share = half // shares
    heads = q.shape[1]
    idx_heads = iq.shape[3]
    idx_scale = (idx_heads * shares * iq.shape[4]) ** (-0.5)

    @pl.when(step == 0)
    def _():
        def sort(r, carry):
            src = pl.ds(pl.multiple_of(r * half, half), half)
            dst = pl.ds(pl.multiple_of(order[r] * half, half), half)
            lat_sorted[dst, :] = lat[src, :]
            idx_sorted[dst, :] = idx[src, :]
            return carry

        lax.fori_loop(0, blocks, sort, 0)
        for e in range(2):
            block = order[2 * ctx + e]
            slot = (block >= blocks // 2).astype(jnp.int32)
            first = block * half + head * share
            logits[...] = jnp.full(logits.shape, -jnp.inf, jnp.float32)
            weights = [
                jnp.broadcast_to(
                    (iw[z, e].astype(jnp.float32) * idx_scale)[:, :, None], (share, idx_heads, 128)
                )
                for z in range(shares)
            ]

            def logit_tile(k, carry):
                cols = pl.ds(pl.multiple_of(k * tile, tile), tile)
                keys = idx_sorted[cols, :]
                total = jnp.zeros((share, tile), jnp.float32)
                for z in range(shares):
                    dots = lax.dot_general(
                        iq[z, e].reshape(share * idx_heads, -1), keys, NT_DIMS,
                        preferred_element_type=jnp.float32,
                    ).reshape(share, idx_heads, tile)
                    parts = [
                        jnp.sum(weights[z] * jnp.maximum(dots[:, :, c : c + 128], 0.0), axis=1)
                        for c in range(0, tile, 128)
                    ]
                    total = total + jnp.concatenate(parts, axis=1)
                shape = (share, tile)
                visible = k * tile + lax.broadcasted_iota(
                    jnp.int32, shape, 1
                ) <= first + lax.broadcasted_iota(jnp.int32, shape, 0)
                logits[:, cols] = jnp.where(visible, total, -jnp.inf)
                return carry

            lax.fori_loop(0, (block * half + half - 1) // tile + 1, logit_tile, 0)
            values = logits[...]
            top = jnp.max(values, axis=1, keepdims=True)
            expo = jnp.exp(values - top)
            norm_sum = jnp.sum(expo, axis=1, keepdims=True)
            probs[pl.ds(pl.multiple_of(slot * share, share), share), :] = expo / norm_sum

    chunk = q.shape[0]
    per_block = half // chunk
    e = step // per_block
    inner = lax.rem(step, per_block)
    block = order[2 * ctx + e]
    slot = (block >= blocks // 2).astype(jnp.int32)
    out_rows = pl.ds(pl.multiple_of(slot * half + inner * chunk, chunk), chunk)
    first = block * half + inner * chunk
    queries = q[...].reshape(chunk * heads, q.shape[2])
    shift = jnp.broadcast_to((norm[...] * log2e)[:, :, None], (chunk, heads, 128))
    count = (block * half + half - 1) // tile + 1

    def score_tile(k, carry):
        cols = pl.ds(pl.multiple_of(k * tile, tile), tile)
        scores = lax.dot_general(
            queries, lat_sorted[cols, :], NT_DIMS, preferred_element_type=jnp.float32
        ).reshape(chunk, heads, tile)
        parts = [
            jnp.sum(
                jnp.exp2(scores[:, :, c : c + 128] * (mla_scale * log2e) - shift), axis=1
            )
            for c in range(0, tile, 128)
        ]
        total = jnp.concatenate(parts, axis=1)
        shape = (chunk, tile)
        visible = k * tile + lax.broadcasted_iota(
            jnp.int32, shape, 1
        ) <= first + lax.broadcasted_iota(jnp.int32, shape, 0)
        sums[out_rows, cols] = jnp.where(visible, total, 0.0)
        return carry

    lax.fori_loop(0, count, score_tile, 0)

    def clear(k, carry):
        cols = pl.ds(pl.multiple_of(k * tile, tile), tile)
        sums[out_rows, cols] = jnp.zeros((chunk, tile), jnp.float32)
        return carry

    lax.fori_loop(count, tiles, clear, 0)


def forward(order, q, norm, lat, idx, iq, iw, shares):
    rows, heads, width = q.shape
    tokens = lat.shape[0]
    half = rows // 2
    share = half // shares
    chunk = 16
    tile = 256
    whole = lambda a: pl.BlockSpec(a.shape, lambda i, o: (0,) * a.ndim)
    return pl.pallas_call(
        functools.partial(forward_kernel, shares, tile),
        out_shape=(
            jax.ShapeDtypeStruct((rows, tokens), jnp.float32),
            jax.ShapeDtypeStruct((2 * share, tokens), jnp.float32),
            jax.ShapeDtypeStruct(idx.shape, idx.dtype),
        ),
        grid_spec=pltpu.PrefetchScalarGridSpec(
            num_scalar_prefetch=1,
            grid=(rows // chunk,),
            in_specs=[
                pl.BlockSpec((chunk, heads, width), lambda i, o: (i, 0, 0)),
                pl.BlockSpec((chunk, heads), lambda i, o: (i, 0)),
                whole(lat), whole(idx), whole(iq), whole(iw),
            ],
            out_specs=[
                pl.BlockSpec((rows, tokens), lambda i, o: (0, 0)),
                pl.BlockSpec((2 * share, tokens), lambda i, o: (0, 0)),
                pl.BlockSpec(idx.shape, lambda i, o: (0, 0)),
            ],
            scratch_shapes=[
                pltpu.VMEM(lat.shape, lat.dtype),
                pltpu.VMEM((share, tokens), jnp.float32),
            ],
        ),
        name="forward",
    )(order, q, norm, lat, idx, iq, iw)


def gradient_kernel(shares, sums, probs, grad, low, high, ls, lr, hs, hr, gs, gr):
    head = lax.axis_index("head")
    rows, tokens = sums.shape
    half = rows // 2
    share = half // shares
    short = tokens // 2
    enter(0, shares)
    sent = []
    for step in range(1, shares):
        peer = lax.rem(head + step, shares)
        start = pl.multiple_of(peer * share, share)
        for copy in (
            remote(
                sums.at[pl.ds(start, share), pl.ds(0, short)], low.at[step], ls.at[step],
                lr.at[step], {"head": peer},
            ),
            remote(
                sums.at[pl.ds(half + start, share)], high.at[step], hs.at[step], hr.at[step],
                {"head": peer},
            ),
        ):
            copy.start()
            sent.append(copy)
    start = pl.multiple_of(head * share, share)
    total_low = sums[pl.ds(start, share), :short]
    total_high = sums[pl.ds(half + start, share), :]
    for step in range(1, shares):
        source = lax.rem(head + shares - step, shares)
        remote(low.at[step], low.at[step], ls.at[step], lr.at[step], {"head": source}).wait_recv()
        total_low = total_low + low[step]
        remote(high.at[step], high.at[step], hs.at[step], hr.at[step], {"head": source}).wait_recv()
        total_high = total_high + high[step]
    row_low = jnp.sum(total_low, axis=1, keepdims=True)
    row_high = jnp.sum(total_high, axis=1, keepdims=True)
    grad[head, 0, :, :short] = (
        loss_scale * (probs[:share, :short] - total_low / row_low)
    ).astype(jnp.bfloat16)
    grad[head, 1] = (loss_scale * (probs[share:, :] - total_high / row_high)).astype(jnp.bfloat16)
    for step in range(1, shares):
        peer = lax.rem(head + step, shares)
        for copy in (
            remote(
                grad.at[head, 0, :, pl.ds(0, short)], grad.at[head, 0, :, pl.ds(0, short)],
                gs.at[0, step], gr.at[0, step], {"head": peer},
            ),
            remote(
                grad.at[head, 1], grad.at[head, 1], gs.at[1, step], gr.at[1, step], {"head": peer}
            ),
        ):
            copy.start()
            sent.append(copy)
    for step in range(1, shares):
        source = lax.rem(head + shares - step, shares)
        slot = grad.at[source, 0, :, pl.ds(0, short)]
        remote(slot, slot, gs.at[0, step], gr.at[0, step], {"head": source}).wait_recv()
        slot = grad.at[source, 1]
        remote(slot, slot, gs.at[1, step], gr.at[1, step], {"head": source}).wait_recv()
    for copy in sent:
        copy.wait_send()


def gradient(sums, probs, shares):
    rows, tokens = sums.shape
    share = rows // 2 // shares
    dma = pltpu.SemaphoreType.DMA
    return pl.pallas_call(
        functools.partial(gradient_kernel, shares),
        out_shape=jax.ShapeDtypeStruct((shares, 2, share, tokens), jnp.bfloat16),
        in_specs=[pl.BlockSpec(memory_space=pltpu.VMEM)] * 2,
        out_specs=pl.BlockSpec(memory_space=pltpu.VMEM),
        scratch_shapes=[
            pltpu.VMEM((shares, share, tokens // 2), jnp.float32),
            pltpu.VMEM((shares, share, tokens), jnp.float32),
            dma((shares,)), dma((shares,)), dma((shares,)), dma((shares,)),
            dma((2, shares)), dma((2, shares)),
        ],
        compiler_params=pltpu.CompilerParams(collective_id=1, has_side_effects=True),
        name="gradient",
    )(sums, probs)


def backward_kernel(shares, tile, order, iq, iw, grad, idx, query_grad, key_grad, total):
    step, steps = pl.program_id(0), pl.num_programs(0)
    ctx = lax.axis_index("ctx")
    blocks = order.shape[0]
    tokens = idx.shape[0]
    half = tokens // blocks
    share, heads, dim = iq.shape
    idx_scale = (heads * shares * dim) ** (-0.5)

    @pl.when(step == 0)
    def _():
        total[...] = jnp.zeros_like(total)

    e = step // shares
    part = lax.rem(step, shares)
    block = order[2 * ctx + e]
    slot = (block >= blocks // 2).astype(jnp.int32)
    queries = iq[...].reshape(share * heads, dim)
    weights = jnp.broadcast_to(
        (iw[...].astype(jnp.float32) * idx_scale)[:, :, None], (share, heads, 128)
    )
    query_grad[...] = jnp.zeros_like(query_grad)

    def grad_tile(k, carry):
        cols = pl.ds(pl.multiple_of(k * tile, tile), tile)
        keys = idx[cols, :]
        dots = lax.dot_general(
            queries, keys, NT_DIMS, preferred_element_type=jnp.float32
        ).reshape(share, heads, tile)
        rate = grad[part, slot, :, cols].astype(jnp.float32)
        parts = [
            jnp.where(
                dots[:, :, c : c + 128] > 0, rate[:, None, c : c + 128] * weights, 0.0
            )
            for c in range(0, tile, 128)
        ]
        coefficient = (
            jnp.concatenate(parts, axis=2).reshape(share * heads, tile).astype(jnp.bfloat16)
        )
        query_grad[...] += jnp.dot(
            coefficient, keys, preferred_element_type=jnp.float32
        ).reshape(share, heads, dim)
        total[cols, :] += lax.dot_general(
            coefficient, queries, TN_DIMS, preferred_element_type=jnp.float32
        )
        return carry

    lax.fori_loop(0, (block * half + half - 1) // tile + 1, grad_tile, 0)

    @pl.when(step == steps - 1)
    def _():
        def store(r, carry):
            dst = pl.ds(pl.multiple_of(r * half, half), half)
            src = pl.ds(pl.multiple_of(order[r] * half, half), half)
            key_grad[dst, :] = total[src, :]
            return carry

        lax.fori_loop(0, blocks, store, 0)


def backward(order, iq, iw, grad, idx, shares):
    rows, heads, dim = iq.shape
    share = rows // 2 // shares
    tile = 256
    return pl.pallas_call(
        functools.partial(backward_kernel, shares, tile),
        out_shape=(
            jax.ShapeDtypeStruct(iq.shape, jnp.float32),
            jax.ShapeDtypeStruct(idx.shape, jnp.float32),
        ),
        grid_spec=pltpu.PrefetchScalarGridSpec(
            num_scalar_prefetch=1,
            grid=(2 * shares,),
            in_specs=[
                pl.BlockSpec((share, heads, dim), lambda i, o: (i, 0, 0)),
                pl.BlockSpec((share, heads), lambda i, o: (i, 0)),
                pl.BlockSpec(grad.shape, lambda i, o: (0, 0, 0, 0)),
                pl.BlockSpec(idx.shape, lambda i, o: (0, 0)),
            ],
            out_specs=[
                pl.BlockSpec((share, heads, dim), lambda i, o: (i, 0, 0)),
                pl.BlockSpec(idx.shape, lambda i, o: (0, 0)),
            ],
            scratch_shapes=[pltpu.VMEM(idx.shape, jnp.float32)],
        ),
        name="backward",
    )(order, iq, iw, grad, idx)


def reduce_kernel(groups, shares, parts, out, near, mid, far, acc, last, ns, nr, ms, mr, fs, fr):
    ctx, head = lax.axis_index("ctx"), lax.axis_index("head")
    group, core = ctx // 2, lax.rem(ctx, 2)
    sibling = group * 2 + 1 - core
    rows = out.shape[0]
    enter(groups, shares)
    sent = []
    for step in [*range(1, groups), 0]:
        peer = lax.rem(group + step, groups)
        copy = remote(
            parts.at[peer * 2 + 1 - core], near.at[step], ns.at[step], nr.at[step], {"ctx": sibling}
        )
        copy.start()
        sent.append(copy)
    for step in range(1, groups):
        peer = lax.rem(group + step, groups)
        remote(near.at[step], near.at[step], ns.at[step], nr.at[step], {"ctx": sibling}).wait_recv()
        acc[step] = parts[peer * 2 + core] + near[step]
        copy = remote(
            acc.at[step], mid.at[step], ms.at[step], mr.at[step], {"ctx": peer * 2 + core}
        )
        copy.start()
        sent.append(copy)
    remote(near.at[0], near.at[0], ns.at[0], nr.at[0], {"ctx": sibling}).wait_recv()
    value = parts[ctx] + near[0]
    for step in range(1, groups):
        remote(mid.at[step], mid.at[step], ms.at[step], mr.at[step], {"ctx": sibling}).wait_recv()
        value = value + mid[step]
    last[...] = value
    for step in range(1, shares):
        peer = lax.rem(head + step, shares)
        copy = remote(
            last.at[pl.ds(pl.multiple_of(peer * rows, rows), rows)], far.at[step], fs.at[step],
            fr.at[step], {"head": peer},
        )
        copy.start()
        sent.append(copy)
    value = last[pl.ds(pl.multiple_of(head * rows, rows), rows), :]
    for step in range(1, shares):
        remote(far.at[step], far.at[step], fs.at[step], fr.at[step], {"head": head}).wait_recv()
        value = value + far[step]
    out[...] = value
    for copy in sent:
        copy.wait_send()


def reduce(parts, cycle, shares):
    groups = cycle // 2
    rows, dim = parts.shape[0] // cycle, parts.shape[1]
    dma = pltpu.SemaphoreType.DMA
    buffer = pltpu.VMEM((groups, rows, dim), jnp.float32)
    return pl.pallas_call(
        functools.partial(reduce_kernel, groups, shares),
        out_shape=jax.ShapeDtypeStruct((rows // shares, dim), jnp.float32),
        in_specs=[pl.BlockSpec(memory_space=pltpu.VMEM)],
        out_specs=pl.BlockSpec(memory_space=pltpu.VMEM),
        scratch_shapes=[
            buffer, buffer, pltpu.VMEM((shares, rows // shares, dim), jnp.float32), buffer,
            pltpu.VMEM((rows, dim), jnp.float32),
            dma((groups,)), dma((groups,)), dma((groups,)), dma((groups,)),
            dma((shares,)), dma((shares,)),
        ],
        compiler_params=pltpu.CompilerParams(collective_id=2, has_side_effects=True),
        name="reduce",
    )(parts.reshape(cycle, rows, dim))


def per_device(
    block_order, query_latent, key_latent, normalizer, indexer_query, indexer_key, indexer_weight
):
    cycle, shares = lax.axis_size("ctx"), lax.axis_size("head")
    lat, idx, iq, iw = gather(
        key_latent, indexer_key, indexer_query, indexer_weight, cycle, shares
    )
    lat = lat.reshape(-1, lat.shape[2])
    idx = idx.reshape(-1, idx.shape[2])
    sums, probs, idx_sorted = forward(
        block_order, query_latent, normalizer, lat, idx, iq, iw, shares
    )
    grad = gradient(sums, probs, shares)
    query_grad, key_parts = backward(
        block_order, indexer_query, indexer_weight, grad, idx_sorted, shares
    )
    return query_grad, reduce(key_parts, cycle, shares)


def solution(mesh):
    return jax.shard_map(
        per_device,
        mesh=mesh,
        in_specs=(
            P(),
            P("ctx", "head", None),
            P("ctx", None),
            P("ctx", "head"),
            P("ctx", "head", None),
            P("ctx", None),
            P("ctx", "head"),
        ),
        out_specs=(P("ctx", "head", None), P(("ctx", "head"), None)),
        check_vma=False,
    )
```

```python
import functools
import math

import jax
import jax.numpy as jnp
from jax import lax
from jax.experimental import pallas as pl
from jax.experimental.pallas import tpu as pltpu
from jax.sharding import PartitionSpec as P

MESH = pl.DeviceIdType.MESH
mla_scale = 192.0 ** (-0.5)
loss_scale = 64.0
log2e = math.log2(math.e)
NT_DIMS = (((1,), (1,)), ((), ()))
TN_DIMS = (((0,), (0,)), ((), ()))


def enter(groups, shares):
    ctx, head = lax.axis_index("ctx"), lax.axis_index("head")
    group, core = ctx // 2, lax.rem(ctx, 2)
    barrier = pltpu.get_barrier_semaphore()
    count = 0
    if groups:
        for step in range(1, groups):
            peer = lax.rem(group + step, groups) * 2 + core
            pl.semaphore_signal(barrier, 1, device_id={"ctx": peer}, device_id_type=MESH)
        pl.semaphore_signal(
            barrier, 1, device_id={"ctx": group * 2 + 1 - core}, device_id_type=MESH
        )
        count += groups
    for step in range(1, shares):
        peer = lax.rem(head + step, shares)
        pl.semaphore_signal(barrier, 1, device_id={"head": peer}, device_id_type=MESH)
    count += shares - 1
    pl.semaphore_wait(barrier, count)


def remote(src, dst, send, recv, device):
    return pltpu.make_async_remote_copy(
        src_ref=src, dst_ref=dst, send_sem=send, recv_sem=recv, device_id=device, device_id_type=MESH
    )


def gather_kernel(
    groups, shares, lat, idx, iq, iw, all_lat, all_idx, iq_recv, iw_recv,
    local, qs, qr, ws, wr, ds, dr, fs, fr,
):
    ctx, head = lax.axis_index("ctx"), lax.axis_index("head")
    group, core = ctx // 2, lax.rem(ctx, 2)
    sibling = group * 2 + 1 - core
    rows = idx.shape[0]
    half = rows // 2
    share = half // shares
    own = [
        pltpu.make_async_copy(lat, all_lat.at[ctx], local.at[0]),
        pltpu.make_async_copy(idx, all_idx.at[ctx], local.at[1]),
    ]
    for e in range(2):
        take = pl.ds(pl.multiple_of(e * half + head * share, share), share)
        own.append(pltpu.make_async_copy(iq.at[take], iq_recv.at[head, e], local.at[2 + e]))
    own.append(pltpu.make_async_copy(iw, iw_recv.at[head], local.at[4]))
    for copy in own:
        copy.start()
    enter(groups, shares)
    sent = []
    for step in range(1, groups):
        peer = lax.rem(group + step, groups) * 2 + core
        for k, (src, dst) in enumerate(((lat, all_lat), (idx, all_idx))):
            copy = remote(src, dst.at[ctx], ds.at[k, step], dr.at[k, step], {"ctx": peer})
            copy.start()
            sent.append(copy)
    for k, (src, dst) in enumerate(((lat, all_lat), (idx, all_idx))):
        copy = remote(src, dst.at[ctx], fs.at[k, 0], fr.at[k, 0], {"ctx": sibling})
        copy.start()
        sent.append(copy)
    for step in range(1, shares):
        peer = lax.rem(head + step, shares)
        for e in range(2):
            take = pl.ds(pl.multiple_of(e * half + peer * share, share), share)
            copy = remote(
                iq.at[take], iq_recv.at[head, e], qs.at[step, e], qr.at[step, e], {"head": peer}
            )
            copy.start()
            sent.append(copy)
        copy = remote(iw, iw_recv.at[head], ws.at[step], wr.at[step], {"head": peer})
        copy.start()
        sent.append(copy)
    for step in range(1, groups):
        source = lax.rem(group + groups - step, groups) * 2 + core
        for k, dst in enumerate((all_lat, all_idx)):
            slot = dst.at[source]
            remote(slot, slot, ds.at[k, step], dr.at[k, step], {"ctx": sibling}).wait_recv()
            copy = remote(slot, slot, fs.at[k, step], fr.at[k, step], {"ctx": sibling})
            copy.start()
            sent.append(copy)
    for step in range(groups):
        source = lax.rem(group + groups - step, groups) * 2 + 1 - core
        for k, dst in enumerate((all_lat, all_idx)):
            slot = dst.at[source]
            remote(slot, slot, fs.at[k, step], fr.at[k, step], {"ctx": sibling}).wait_recv()
    for step in range(1, shares):
        source = lax.rem(head + shares - step, shares)
        for e in range(2):
            slot = iq_recv.at[source, e]
            remote(slot, slot, qs.at[step, e], qr.at[step, e], {"head": source}).wait_recv()
        slot = iw_recv.at[source]
        remote(slot, slot, ws.at[step], wr.at[step], {"head": source}).wait_recv()
    for copy in sent:
        copy.wait_send()
    for copy in own:
        copy.wait()


def gather(lat, idx, iq, iw, cycle, shares):
    groups = cycle // 2
    rows = idx.shape[0]
    share = rows // 2 // shares
    dma = pltpu.SemaphoreType.DMA
    return pl.pallas_call(
        functools.partial(gather_kernel, groups, shares),
        out_shape=(
            jax.ShapeDtypeStruct((cycle,) + lat.shape, lat.dtype),
            jax.ShapeDtypeStruct((cycle,) + idx.shape, idx.dtype),
            jax.ShapeDtypeStruct((shares, 2, share) + iq.shape[1:], iq.dtype),
            jax.ShapeDtypeStruct((shares,) + iw.shape, iw.dtype),
        ),
        in_specs=[pl.BlockSpec(memory_space=pl.ANY)] * 4,
        out_specs=[pl.BlockSpec(memory_space=pltpu.VMEM)] * 4,
        scratch_shapes=[
            dma((5,)),
            dma((shares, 2)), dma((shares, 2)), dma((shares,)), dma((shares,)),
            dma((2, groups)), dma((2, groups)), dma((2, groups)), dma((2, groups)),
        ],
        compiler_params=pltpu.CompilerParams(collective_id=0, has_side_effects=True),
        name="gather",
    )(lat, idx, iq, iw)


def forward_kernel(
    shares, tile, order, q, norm, lat, idx, iq, iw, sums, probs, idx_sorted, lat_sorted, logits, acc
):
    step, steps = pl.program_id(0), pl.num_programs(0)
    ctx, head = lax.axis_index("ctx"), lax.axis_index("head")
    blocks = order.shape[0]
    tokens = idx.shape[0]
    half = tokens // blocks
    rows = 2 * half
    tiles = tokens // tile
    share = half // shares
    idx_heads = iq.shape[3]
    idx_scale = (idx_heads * shares * iq.shape[4]) ** (-0.5)

    @pl.when(step == 0)
    def _():
        acc[...] = jnp.zeros_like(acc)

        def sort(c, carry):
            pair = lat[c].T
            for e in range(2):
                src = pl.ds(pl.multiple_of((2 * c + e) * half, half), half)
                dst = pl.ds(pl.multiple_of(order[2 * c + e] * half, half), half)
                lat_sorted[dst, :] = pair[e * half : (e + 1) * half]
                idx_sorted[dst, :] = idx[src, :]
            return carry

        lax.fori_loop(0, blocks // 2, sort, 0)
        for e in range(2):
            block = order[2 * ctx + e]
            slot = (block >= blocks // 2).astype(jnp.int32)
            first = block * half + head * share
            logits[...] = jnp.full(logits.shape, -jnp.inf, jnp.float32)
            weights = []
            for z in range(shares):
                flat = iw[z].astype(jnp.float32).T * idx_scale
                flat = sum(
                    jnp.where(head == y, flat[e * half + y * share : e * half + (y + 1) * share], 0.0)
                    for y in range(shares)
                )
                weights.append(jnp.broadcast_to(flat[:, :, None], (share, idx_heads, 128)))

            def logit_tile(k, carry):
                cols = pl.ds(pl.multiple_of(k * tile, tile), tile)
                keys = idx_sorted[cols, :]
                total = jnp.zeros((share, tile), jnp.float32)
                for z in range(shares):
                    dots = lax.dot_general(
                        iq[z, e].reshape(share * idx_heads, -1), keys, NT_DIMS,
                        preferred_element_type=jnp.float32,
                    ).reshape(share, idx_heads, tile)
                    parts = [
                        jnp.sum(weights[z] * jnp.maximum(dots[:, :, c : c + 128], 0.0), axis=1)
                        for c in range(0, tile, 128)
                    ]
                    total = total + jnp.concatenate(parts, axis=1)
                shape = (share, tile)
                visible = k * tile + lax.broadcasted_iota(
                    jnp.int32, shape, 1
                ) <= first + lax.broadcasted_iota(jnp.int32, shape, 0)
                logits[:, cols] = jnp.where(visible, total, -jnp.inf)
                return carry

            lax.fori_loop(0, (block * half + half - 1) // tile + 1, logit_tile, 0)
            values = logits[...]
            top = jnp.max(values, axis=1, keepdims=True)
            expo = jnp.exp(values - top)
            norm_sum = jnp.sum(expo, axis=1, keepdims=True)
            probs[pl.ds(pl.multiple_of(slot * share, share), share), :] = expo / norm_sum

    group = q.shape[0]
    shift = norm[pl.ds(pl.multiple_of(step * group, group), group), :] * log2e

    def score_tile(k, carry):
        keys = lat_sorted[pl.ds(pl.multiple_of(k * tile, tile), tile), :]
        total = acc[pl.ds(pl.multiple_of(k * tile, tile), tile), :]
        for h in range(0, group, 2):
            scores = jnp.dot(
                keys, jnp.concatenate((q[h], q[h + 1]), axis=1), preferred_element_type=jnp.float32
            ) * (mla_scale * log2e)
            total = total + jnp.exp2(scores[:, :rows] - shift[h : h + 1])
            total = total + jnp.exp2(scores[:, rows:] - shift[h + 1 : h + 2])
        acc[pl.ds(pl.multiple_of(k * tile, tile), tile), :] = total
        return carry

    lax.fori_loop(0, tiles, score_tile, 0)

    @pl.when(step == steps - 1)
    def _():
        def finish(k, carry):
            cols = pl.ds(pl.multiple_of(k * tile, tile), tile)
            total = acc[cols, :].T
            shape = (half, tile)
            for e in range(2):
                block = order[2 * ctx + e]
                slot = (block >= blocks // 2).astype(jnp.int32)
                visible = k * tile + lax.broadcasted_iota(
                    jnp.int32, shape, 1
                ) <= block * half + lax.broadcasted_iota(jnp.int32, shape, 0)
                sums[pl.ds(pl.multiple_of(slot * half, half), half), cols] = jnp.where(
                    visible, total[e * half : (e + 1) * half], 0.0
                )
            return carry

        lax.fori_loop(0, tiles, finish, 0)


def forward(order, q, norm, lat, idx, iq, iw, shares):
    heads, width, rows = q.shape
    tokens = idx.shape[0]
    half = rows // 2
    share = half // shares
    group = 8
    tile = 256
    whole = lambda a: pl.BlockSpec(a.shape, lambda i, o: (0,) * a.ndim)
    return pl.pallas_call(
        functools.partial(forward_kernel, shares, tile),
        out_shape=(
            jax.ShapeDtypeStruct((rows, tokens), jnp.float32),
            jax.ShapeDtypeStruct((2 * share, tokens), jnp.float32),
            jax.ShapeDtypeStruct(idx.shape, idx.dtype),
        ),
        grid_spec=pltpu.PrefetchScalarGridSpec(
            num_scalar_prefetch=1,
            grid=(heads // group,),
            in_specs=[
                pl.BlockSpec((group, width, rows), lambda i, o: (i, 0, 0)),
                whole(norm), whole(lat), whole(idx), whole(iq), whole(iw),
            ],
            out_specs=[
                pl.BlockSpec((rows, tokens), lambda i, o: (0, 0)),
                pl.BlockSpec((2 * share, tokens), lambda i, o: (0, 0)),
                pl.BlockSpec(idx.shape, lambda i, o: (0, 0)),
            ],
            scratch_shapes=[
                pltpu.VMEM((tokens, width), lat.dtype),
                pltpu.VMEM((share, tokens), jnp.float32),
                pltpu.VMEM((tokens, rows), jnp.float32),
            ],
        ),
        name="forward",
    )(order, q, norm, lat, idx, iq, iw)


def gradient_kernel(shares, sums, probs, grad, short_sums, low, high, ls, lr, hs, hr, gs, gr):
    head = lax.axis_index("head")
    rows, tokens = sums.shape
    half = rows // 2
    share = half // shares
    short = tokens // 2
    short_sums[...] = sums[...].astype(jnp.bfloat16)
    enter(0, shares)
    sent = []
    for step in range(1, shares):
        peer = lax.rem(head + step, shares)
        start = pl.multiple_of(peer * share, share)
        for copy in (
            remote(
                short_sums.at[pl.ds(start, share), pl.ds(0, short)], low.at[step], ls.at[step],
                lr.at[step], {"head": peer},
            ),
            remote(
                short_sums.at[pl.ds(half + start, share)], high.at[step], hs.at[step], hr.at[step],
                {"head": peer},
            ),
        ):
            copy.start()
            sent.append(copy)
    start = pl.multiple_of(head * share, share)
    total_low = sums[pl.ds(start, share), :short]
    total_high = sums[pl.ds(half + start, share), :]
    for step in range(1, shares):
        source = lax.rem(head + shares - step, shares)
        remote(low.at[step], low.at[step], ls.at[step], lr.at[step], {"head": source}).wait_recv()
        total_low = total_low + low[step].astype(jnp.float32)
        remote(high.at[step], high.at[step], hs.at[step], hr.at[step], {"head": source}).wait_recv()
        total_high = total_high + high[step].astype(jnp.float32)
    row_low = jnp.sum(total_low, axis=1, keepdims=True)
    row_high = jnp.sum(total_high, axis=1, keepdims=True)
    grad[head, 0, :, :short] = (
        loss_scale * (probs[:share, :short] - total_low / row_low)
    ).astype(jnp.bfloat16)
    grad[head, 1] = (loss_scale * (probs[share:, :] - total_high / row_high)).astype(jnp.bfloat16)
    for step in range(1, shares):
        peer = lax.rem(head + step, shares)
        for copy in (
            remote(
                grad.at[head, 0, :, pl.ds(0, short)], grad.at[head, 0, :, pl.ds(0, short)],
                gs.at[0, step], gr.at[0, step], {"head": peer},
            ),
            remote(
                grad.at[head, 1], grad.at[head, 1], gs.at[1, step], gr.at[1, step], {"head": peer}
            ),
        ):
            copy.start()
            sent.append(copy)
    for step in range(1, shares):
        source = lax.rem(head + shares - step, shares)
        slot = grad.at[source, 0, :, pl.ds(0, short)]
        remote(slot, slot, gs.at[0, step], gr.at[0, step], {"head": source}).wait_recv()
        slot = grad.at[source, 1]
        remote(slot, slot, gs.at[1, step], gr.at[1, step], {"head": source}).wait_recv()
    for copy in sent:
        copy.wait_send()


def gradient(sums, probs, shares):
    rows, tokens = sums.shape
    share = rows // 2 // shares
    dma = pltpu.SemaphoreType.DMA
    return pl.pallas_call(
        functools.partial(gradient_kernel, shares),
        out_shape=jax.ShapeDtypeStruct((shares, 2, share, tokens), jnp.bfloat16),
        in_specs=[pl.BlockSpec(memory_space=pltpu.VMEM)] * 2,
        out_specs=pl.BlockSpec(memory_space=pltpu.VMEM),
        scratch_shapes=[
            pltpu.VMEM(sums.shape, jnp.bfloat16),
            pltpu.VMEM((shares, share, tokens // 2), jnp.bfloat16),
            pltpu.VMEM((shares, share, tokens), jnp.bfloat16),
            dma((shares,)), dma((shares,)), dma((shares,)), dma((shares,)),
            dma((2, shares)), dma((2, shares)),
        ],
        compiler_params=pltpu.CompilerParams(collective_id=1, has_side_effects=True),
        name="gradient",
    )(sums, probs)


def backward_kernel(shares, tile, order, iq, iw, grad, idx, query_grad, key_grad, total, scaled):
    step, steps = pl.program_id(0), pl.num_programs(0)
    ctx = lax.axis_index("ctx")
    blocks = order.shape[0]
    tokens = idx.shape[0]
    half = tokens // blocks
    share, heads, dim = iq.shape
    idx_scale = (heads * shares * dim) ** (-0.5)

    @pl.when(step == 0)
    def _():
        total[...] = jnp.zeros_like(total)
        scaled[...] = iw[...].astype(jnp.float32).T * idx_scale

    e = step // shares
    part = lax.rem(step, shares)
    block = order[2 * ctx + e]
    slot = (block >= blocks // 2).astype(jnp.int32)
    queries = iq[...].reshape(share * heads, dim)
    weights = jnp.broadcast_to(
        scaled[pl.ds(pl.multiple_of(step * share, share), share), :][:, :, None], (share, heads, 128)
    )
    query_grad[...] = jnp.zeros_like(query_grad)

    def grad_tile(k, carry):
        cols = pl.ds(pl.multiple_of(k * tile, tile), tile)
        keys = idx[cols, :]
        dots = lax.dot_general(
            queries, keys, NT_DIMS, preferred_element_type=jnp.float32
        ).reshape(share, heads, tile)
        rate = grad[part, slot, :, cols].astype(jnp.float32)
        parts = [
            jnp.where(
                dots[:, :, c : c + 128] > 0, rate[:, None, c : c + 128] * weights, 0.0
            )
            for c in range(0, tile, 128)
        ]
        coefficient = (
            jnp.concatenate(parts, axis=2).reshape(share * heads, tile).astype(jnp.bfloat16)
        )
        query_grad[...] += jnp.dot(
            coefficient, keys, preferred_element_type=jnp.float32
        ).reshape(share, heads, dim)
        total[cols, :] += lax.dot_general(
            coefficient, queries, TN_DIMS, preferred_element_type=jnp.float32
        )
        return carry

    lax.fori_loop(0, (block * half + half - 1) // tile + 1, grad_tile, 0)

    @pl.when(step == steps - 1)
    def _():
        def store(r, carry):
            dst = pl.ds(pl.multiple_of(r * half, half), half)
            src = pl.ds(pl.multiple_of(order[r] * half, half), half)
            key_grad[dst, :] = total[src, :]
            return carry

        lax.fori_loop(0, blocks, store, 0)


def backward(order, iq, iw, grad, idx, shares):
    rows, heads, dim = iq.shape
    share = rows // 2 // shares
    tile = 256
    return pl.pallas_call(
        functools.partial(backward_kernel, shares, tile),
        out_shape=(
            jax.ShapeDtypeStruct(iq.shape, jnp.float32),
            jax.ShapeDtypeStruct(idx.shape, jnp.float32),
        ),
        grid_spec=pltpu.PrefetchScalarGridSpec(
            num_scalar_prefetch=1,
            grid=(2 * shares,),
            in_specs=[
                pl.BlockSpec((share, heads, dim), lambda i, o: (i, 0, 0)),
                pl.BlockSpec(iw.shape, lambda i, o: (0, 0)),
                pl.BlockSpec(grad.shape, lambda i, o: (0, 0, 0, 0)),
                pl.BlockSpec(idx.shape, lambda i, o: (0, 0)),
            ],
            out_specs=[
                pl.BlockSpec((share, heads, dim), lambda i, o: (i, 0, 0)),
                pl.BlockSpec(idx.shape, lambda i, o: (0, 0)),
            ],
            scratch_shapes=[
                pltpu.VMEM(idx.shape, jnp.float32), pltpu.VMEM((rows, heads), jnp.float32)
            ],
        ),
        name="backward",
    )(order, iq, iw, grad, idx)


def reduce_kernel(groups, shares, parts, out, near, mid, far, acc, last, ns, nr, ms, mr, fs, fr):
    ctx, head = lax.axis_index("ctx"), lax.axis_index("head")
    group, core = ctx // 2, lax.rem(ctx, 2)
    sibling = group * 2 + 1 - core
    rows = out.shape[0]
    enter(groups, shares)
    sent = []
    for step in [*range(1, groups), 0]:
        peer = lax.rem(group + step, groups)
        copy = remote(
            parts.at[peer * 2 + 1 - core], near.at[step], ns.at[step], nr.at[step], {"ctx": sibling}
        )
        copy.start()
        sent.append(copy)
    for step in range(1, groups):
        peer = lax.rem(group + step, groups)
        remote(near.at[step], near.at[step], ns.at[step], nr.at[step], {"ctx": sibling}).wait_recv()
        acc[step] = parts[peer * 2 + core] + near[step]
        copy = remote(
            acc.at[step], mid.at[step], ms.at[step], mr.at[step], {"ctx": peer * 2 + core}
        )
        copy.start()
        sent.append(copy)
    remote(near.at[0], near.at[0], ns.at[0], nr.at[0], {"ctx": sibling}).wait_recv()
    value = parts[ctx] + near[0]
    for step in range(1, groups):
        remote(mid.at[step], mid.at[step], ms.at[step], mr.at[step], {"ctx": sibling}).wait_recv()
        value = value + mid[step]
    last[...] = value
    for step in range(1, shares):
        peer = lax.rem(head + step, shares)
        copy = remote(
            last.at[pl.ds(pl.multiple_of(peer * rows, rows), rows)], far.at[step], fs.at[step],
            fr.at[step], {"head": peer},
        )
        copy.start()
        sent.append(copy)
    value = last[pl.ds(pl.multiple_of(head * rows, rows), rows), :]
    for step in range(1, shares):
        remote(far.at[step], far.at[step], fs.at[step], fr.at[step], {"head": head}).wait_recv()
        value = value + far[step]
    out[...] = value
    for copy in sent:
        copy.wait_send()


def reduce(parts, cycle, shares):
    groups = cycle // 2
    rows, dim = parts.shape[0] // cycle, parts.shape[1]
    dma = pltpu.SemaphoreType.DMA
    buffer = pltpu.VMEM((groups, rows, dim), jnp.float32)
    return pl.pallas_call(
        functools.partial(reduce_kernel, groups, shares),
        out_shape=jax.ShapeDtypeStruct((rows // shares, dim), jnp.float32),
        in_specs=[pl.BlockSpec(memory_space=pltpu.VMEM)],
        out_specs=pl.BlockSpec(memory_space=pltpu.VMEM),
        scratch_shapes=[
            buffer, buffer, pltpu.VMEM((shares, rows // shares, dim), jnp.float32), buffer,
            pltpu.VMEM((rows, dim), jnp.float32),
            dma((groups,)), dma((groups,)), dma((groups,)), dma((groups,)),
            dma((shares,)), dma((shares,)),
        ],
        compiler_params=pltpu.CompilerParams(collective_id=2, has_side_effects=True),
        name="reduce",
    )(parts.reshape(cycle, rows, dim))


def per_device(
    block_order, query_latent, key_latent, normalizer, indexer_query, indexer_key, indexer_weight
):
    cycle, shares = lax.axis_size("ctx"), lax.axis_size("head")
    weight = indexer_weight.T
    lat, idx, iq, iw = gather(key_latent.T, indexer_key, indexer_query, weight, cycle, shares)
    idx = idx.reshape(-1, idx.shape[2])
    sums, probs, idx_sorted = forward(
        block_order, query_latent.transpose(1, 2, 0), normalizer.T, lat, idx, iq, iw, shares
    )
    grad = gradient(sums, probs, shares)
    query_grad, key_parts = backward(
        block_order, indexer_query, weight, grad, idx_sorted, shares
    )
    return query_grad, reduce(key_parts, cycle, shares)


def solution(mesh):
    return jax.shard_map(
        per_device,
        mesh=mesh,
        in_specs=(
            P(),
            P("ctx", "head", None),
            P("ctx", None),
            P("ctx", "head"),
            P("ctx", "head", None),
            P("ctx", None),
            P("ctx", "head"),
        ),
        out_specs=(P("ctx", "head", None), P(("ctx", "head"), None)),
        check_vma=False,
    )
```

```python
import functools
import math

import jax
import jax.numpy as jnp
from jax import lax
from jax.experimental import pallas as pl
from jax.experimental.pallas import tpu as pltpu
from jax.sharding import PartitionSpec as P

MESH = pl.DeviceIdType.MESH
mla_scale = 192.0 ** (-0.5)
loss_scale = 64.0
log2e = math.log2(math.e)
NT_DIMS = (((1,), (1,)), ((), ()))
TN_DIMS = (((0,), (0,)), ((), ()))


def enter(groups, shares):
    ctx, head = lax.axis_index("ctx"), lax.axis_index("head")
    group, core = ctx // 2, lax.rem(ctx, 2)
    barrier = pltpu.get_barrier_semaphore()
    count = 0
    if groups:
        for step in range(1, groups):
            peer = lax.rem(group + step, groups) * 2 + core
            pl.semaphore_signal(barrier, 1, device_id={"ctx": peer}, device_id_type=MESH)
        pl.semaphore_signal(
            barrier, 1, device_id={"ctx": group * 2 + 1 - core}, device_id_type=MESH
        )
        count += groups
    for step in range(1, shares):
        peer = lax.rem(head + step, shares)
        pl.semaphore_signal(barrier, 1, device_id={"head": peer}, device_id_type=MESH)
    count += shares - 1
    pl.semaphore_wait(barrier, count)


def remote(src, dst, send, recv, device):
    return pltpu.make_async_remote_copy(
        src_ref=src, dst_ref=dst, send_sem=send, recv_sem=recv, device_id=device, device_id_type=MESH
    )


def gather_kernel(
    groups, shares, lat, idx, iq, iw, q_far, norm, acc, all_idx, iq_recv, iw_recv,
    all_lat, q, keys, local, qs, qr, ws, wr, ds, dr, fs, fr,
):
    ctx, head = lax.axis_index("ctx"), lax.axis_index("head")
    group, core = ctx // 2, lax.rem(ctx, 2)
    sibling = group * 2 + 1 - core
    rows = idx.shape[0]
    half = rows // 2
    share = half // shares
    own = [
        pltpu.make_async_copy(lat, all_lat.at[ctx], local.at[0]),
        pltpu.make_async_copy(idx, all_idx.at[ctx], local.at[1]),
    ]
    for e in range(2):
        take = pl.ds(pl.multiple_of(e * half + head * share, share), share)
        own.append(pltpu.make_async_copy(iq.at[take], iq_recv.at[head, e], local.at[2 + e]))
    own.append(pltpu.make_async_copy(iw, iw_recv.at[head], local.at[4]))
    own.append(pltpu.make_async_copy(q_far, q, local.at[5]))
    for copy in own:
        copy.start()
    heads, bundle = q.shape[0], 8

    def score(source):
        keys[...] = jnp.concatenate((all_lat[2 * source], all_lat[2 * source + 1]), axis=1).T

        def body(i, total):
            shift = norm[pl.ds(pl.multiple_of(i * bundle, bundle), bundle), :] * log2e
            for h in range(0, bundle, 2):
                pair = jnp.concatenate((q[i * bundle + h], q[i * bundle + h + 1]), axis=1)
                scores = jnp.dot(keys[...], pair, preferred_element_type=jnp.float32) * (
                    mla_scale * log2e
                )
                total = total + jnp.exp2(scores[:, :rows] - shift[h : h + 1])
                total = total + jnp.exp2(scores[:, rows:] - shift[h + 1 : h + 2])
            return total

        acc[source] = lax.fori_loop(
            0, heads // bundle, body, jnp.zeros((2 * rows, rows), jnp.float32)
        )

    enter(groups, shares)
    sent = []
    for step in range(1, groups):
        peer = lax.rem(group + step, groups) * 2 + core
        for k, (src, dst) in enumerate(((lat, all_lat), (idx, all_idx))):
            copy = remote(src, dst.at[ctx], ds.at[k, step], dr.at[k, step], {"ctx": peer})
            copy.start()
            sent.append(copy)
    for k, (src, dst) in enumerate(((lat, all_lat), (idx, all_idx))):
        copy = remote(src, dst.at[ctx], fs.at[k, 0], fr.at[k, 0], {"ctx": sibling})
        copy.start()
        sent.append(copy)
    for step in range(1, shares):
        peer = lax.rem(head + step, shares)
        for e in range(2):
            take = pl.ds(pl.multiple_of(e * half + peer * share, share), share)
            copy = remote(
                iq.at[take], iq_recv.at[head, e], qs.at[step, e], qr.at[step, e], {"head": peer}
            )
            copy.start()
            sent.append(copy)
        copy = remote(iw, iw_recv.at[head], ws.at[step], wr.at[step], {"head": peer})
        copy.start()
        sent.append(copy)
    slot = all_lat.at[sibling]
    remote(slot, slot, fs.at[0, 0], fr.at[0, 0], {"ctx": sibling}).wait_recv()
    own[0].wait()
    own[-1].wait()
    score(group)
    for step in range(1, groups):
        source = lax.rem(group + groups - step, groups) * 2 + core
        for k, dst in enumerate((all_lat, all_idx)):
            slot = dst.at[source]
            remote(slot, slot, ds.at[k, step], dr.at[k, step], {"ctx": sibling}).wait_recv()
            copy = remote(slot, slot, fs.at[k, step], fr.at[k, step], {"ctx": sibling})
            copy.start()
            sent.append(copy)
    slot = all_idx.at[sibling]
    remote(slot, slot, fs.at[1, 0], fr.at[1, 0], {"ctx": sibling}).wait_recv()
    for step in range(1, groups):
        source = lax.rem(group + groups - step, groups)
        for k, dst in enumerate((all_lat, all_idx)):
            slot = dst.at[source * 2 + 1 - core]
            remote(slot, slot, fs.at[k, step], fr.at[k, step], {"ctx": sibling}).wait_recv()
        score(source)
    for step in range(1, shares):
        source = lax.rem(head + shares - step, shares)
        for e in range(2):
            slot = iq_recv.at[source, e]
            remote(slot, slot, qs.at[step, e], qr.at[step, e], {"head": source}).wait_recv()
        slot = iw_recv.at[source]
        remote(slot, slot, ws.at[step], wr.at[step], {"head": source}).wait_recv()
    for copy in sent:
        copy.wait_send()
    for copy in own[1:-1]:
        copy.wait()


def gather(lat, idx, iq, iw, q, norm, cycle, shares):
    groups = cycle // 2
    rows = idx.shape[0]
    share = rows // 2 // shares
    dma = pltpu.SemaphoreType.DMA
    return pl.pallas_call(
        functools.partial(gather_kernel, groups, shares),
        out_shape=(
            jax.ShapeDtypeStruct((groups, 2 * rows, rows), jnp.float32),
            jax.ShapeDtypeStruct((cycle,) + idx.shape, idx.dtype),
            jax.ShapeDtypeStruct((shares, 2, share) + iq.shape[1:], iq.dtype),
            jax.ShapeDtypeStruct((shares,) + iw.shape, iw.dtype),
        ),
        in_specs=[pl.BlockSpec(memory_space=pl.ANY)] * 5
        + [pl.BlockSpec(memory_space=pltpu.VMEM)],
        out_specs=[pl.BlockSpec(memory_space=pltpu.VMEM)] * 4,
        scratch_shapes=[
            pltpu.VMEM((cycle,) + lat.shape, lat.dtype),
            pltpu.VMEM(q.shape, q.dtype),
            pltpu.VMEM((2 * rows, lat.shape[0]), lat.dtype),
            dma((6,)),
            dma((shares, 2)), dma((shares, 2)), dma((shares,)), dma((shares,)),
            dma((2, groups)), dma((2, groups)), dma((2, groups)), dma((2, groups)),
        ],
        compiler_params=pltpu.CompilerParams(collective_id=0, has_side_effects=True),
        name="gather",
    )(lat, idx, iq, iw, q, norm)


def forward_kernel(
    shares, tile, order, lat, idx, iq, iw, sums, probs, idx_sorted, logits, acc
):
    ctx, head = lax.axis_index("ctx"), lax.axis_index("head")
    blocks = order.shape[0]
    tokens = idx.shape[0]
    half = tokens // blocks
    rows = 2 * half
    tiles = tokens // tile
    share = half // shares
    idx_heads = iq.shape[3]
    idx_scale = (idx_heads * shares * iq.shape[4]) ** (-0.5)

    def sort(c, carry):
        for e in range(2):
            src = pl.ds(pl.multiple_of((2 * c + e) * half, half), half)
            dst = pl.ds(pl.multiple_of(order[2 * c + e] * half, half), half)
            acc[dst, :] = lat[src, :]
            idx_sorted[dst, :] = idx[src, :]
        return carry

    lax.fori_loop(0, blocks // 2, sort, 0)
    for e in range(2):
        block = order[2 * ctx + e]
        slot = (block >= blocks // 2).astype(jnp.int32)
        first = block * half + head * share
        logits[...] = jnp.full(logits.shape, -jnp.inf, jnp.float32)
        weights = []
        for z in range(shares):
            flat = iw[z].astype(jnp.float32).T * idx_scale
            flat = sum(
                jnp.where(head == y, flat[e * half + y * share : e * half + (y + 1) * share], 0.0)
                for y in range(shares)
            )
            weights.append(jnp.broadcast_to(flat[:, :, None], (share, idx_heads, 128)))

        def logit_tile(k, carry):
            cols = pl.ds(pl.multiple_of(k * tile, tile), tile)
            keys = idx_sorted[cols, :]
            total = jnp.zeros((share, tile), jnp.float32)
            for z in range(shares):
                dots = lax.dot_general(
                    iq[z, e].reshape(share * idx_heads, -1), keys, NT_DIMS,
                    preferred_element_type=jnp.float32,
                ).reshape(share, idx_heads, tile)
                parts = [
                    jnp.sum(weights[z] * jnp.maximum(dots[:, :, c : c + 128], 0.0), axis=1)
                    for c in range(0, tile, 128)
                ]
                total = total + jnp.concatenate(parts, axis=1)
            shape = (share, tile)
            visible = k * tile + lax.broadcasted_iota(
                jnp.int32, shape, 1
            ) <= first + lax.broadcasted_iota(jnp.int32, shape, 0)
            logits[:, cols] = jnp.where(visible, total, -jnp.inf)
            return carry

        lax.fori_loop(0, (block * half + half - 1) // tile + 1, logit_tile, 0)
        values = logits[...]
        top = jnp.max(values, axis=1, keepdims=True)
        expo = jnp.exp(values - top)
        norm_sum = jnp.sum(expo, axis=1, keepdims=True)
        probs[pl.ds(pl.multiple_of(slot * share, share), share), :] = expo / norm_sum

    def finish(k, carry):
        cols = pl.ds(pl.multiple_of(k * tile, tile), tile)
        total = acc[cols, :].T
        shape = (half, tile)
        for e in range(2):
            block = order[2 * ctx + e]
            slot = (block >= blocks // 2).astype(jnp.int32)
            visible = k * tile + lax.broadcasted_iota(
                jnp.int32, shape, 1
            ) <= block * half + lax.broadcasted_iota(jnp.int32, shape, 0)
            sums[pl.ds(pl.multiple_of(slot * half, half), half), cols] = jnp.where(
                visible, total[e * half : (e + 1) * half], 0.0
            )
        return carry

    lax.fori_loop(0, tiles, finish, 0)


def forward(order, lat, idx, iq, iw, shares):
    tokens, rows = lat.shape
    share = rows // 2 // shares
    vmem = pl.BlockSpec(memory_space=pltpu.VMEM)
    return pl.pallas_call(
        functools.partial(forward_kernel, shares, 256),
        out_shape=(
            jax.ShapeDtypeStruct((rows, tokens), jnp.float32),
            jax.ShapeDtypeStruct((2 * share, tokens), jnp.float32),
            jax.ShapeDtypeStruct(idx.shape, idx.dtype),
        ),
        in_specs=[pl.BlockSpec(memory_space=pltpu.SMEM)] + [vmem] * 4,
        out_specs=[vmem] * 3,
        scratch_shapes=[
            pltpu.VMEM((share, tokens), jnp.float32),
            pltpu.VMEM((tokens, rows), jnp.float32),
        ],
        name="forward",
    )(order, lat, idx, iq, iw)


def gradient_kernel(shares, sums, probs, grad, short_sums, low, high, ls, lr, hs, hr, gs, gr):
    head = lax.axis_index("head")
    rows, tokens = sums.shape
    half = rows // 2
    share = half // shares
    short = tokens // 2
    short_sums[...] = sums[...].astype(jnp.bfloat16)
    enter(0, shares)
    sent = []
    for step in range(1, shares):
        peer = lax.rem(head + step, shares)
        start = pl.multiple_of(peer * share, share)
        for copy in (
            remote(
                short_sums.at[pl.ds(start, share), pl.ds(0, short)], low.at[step], ls.at[step],
                lr.at[step], {"head": peer},
            ),
            remote(
                short_sums.at[pl.ds(half + start, share)], high.at[step], hs.at[step], hr.at[step],
                {"head": peer},
            ),
        ):
            copy.start()
            sent.append(copy)
    start = pl.multiple_of(head * share, share)
    total_low = sums[pl.ds(start, share), :short]
    total_high = sums[pl.ds(half + start, share), :]
    for step in range(1, shares):
        source = lax.rem(head + shares - step, shares)
        remote(low.at[step], low.at[step], ls.at[step], lr.at[step], {"head": source}).wait_recv()
        total_low = total_low + low[step].astype(jnp.float32)
        remote(high.at[step], high.at[step], hs.at[step], hr.at[step], {"head": source}).wait_recv()
        total_high = total_high + high[step].astype(jnp.float32)
    row_low = jnp.sum(total_low, axis=1, keepdims=True)
    row_high = jnp.sum(total_high, axis=1, keepdims=True)
    grad[head, 0, :, :short] = (
        loss_scale * (probs[:share, :short] - total_low / row_low)
    ).astype(jnp.bfloat16)
    grad[head, 1] = (loss_scale * (probs[share:, :] - total_high / row_high)).astype(jnp.bfloat16)
    for step in range(1, shares):
        peer = lax.rem(head + step, shares)
        for copy in (
            remote(
                grad.at[head, 0, :, pl.ds(0, short)], grad.at[head, 0, :, pl.ds(0, short)],
                gs.at[0, step], gr.at[0, step], {"head": peer},
            ),
            remote(
                grad.at[head, 1], grad.at[head, 1], gs.at[1, step], gr.at[1, step], {"head": peer}
            ),
        ):
            copy.start()
            sent.append(copy)
    for step in range(1, shares):
        source = lax.rem(head + shares - step, shares)
        slot = grad.at[source, 0, :, pl.ds(0, short)]
        remote(slot, slot, gs.at[0, step], gr.at[0, step], {"head": source}).wait_recv()
        slot = grad.at[source, 1]
        remote(slot, slot, gs.at[1, step], gr.at[1, step], {"head": source}).wait_recv()
    for copy in sent:
        copy.wait_send()


def gradient(sums, probs, shares):
    rows, tokens = sums.shape
    share = rows // 2 // shares
    dma = pltpu.SemaphoreType.DMA
    return pl.pallas_call(
        functools.partial(gradient_kernel, shares),
        out_shape=jax.ShapeDtypeStruct((shares, 2, share, tokens), jnp.bfloat16),
        in_specs=[pl.BlockSpec(memory_space=pltpu.VMEM)] * 2,
        out_specs=pl.BlockSpec(memory_space=pltpu.VMEM),
        scratch_shapes=[
            pltpu.VMEM(sums.shape, jnp.bfloat16),
            pltpu.VMEM((shares, share, tokens // 2), jnp.bfloat16),
            pltpu.VMEM((shares, share, tokens), jnp.bfloat16),
            dma((shares,)), dma((shares,)), dma((shares,)), dma((shares,)),
            dma((2, shares)), dma((2, shares)),
        ],
        compiler_params=pltpu.CompilerParams(collective_id=1, has_side_effects=True),
        name="gradient",
    )(sums, probs)


def backward_kernel(shares, tile, order, iq, iw, grad, idx, query_grad, key_grad, total, scaled):
    step, steps = pl.program_id(0), pl.num_programs(0)
    ctx = lax.axis_index("ctx")
    blocks = order.shape[0]
    tokens = idx.shape[0]
    half = tokens // blocks
    share, heads, dim = iq.shape
    idx_scale = (heads * shares * dim) ** (-0.5)

    @pl.when(step == 0)
    def _():
        total[...] = jnp.zeros_like(total)
        scaled[...] = iw[...].astype(jnp.float32).T * idx_scale

    e = step // shares
    part = lax.rem(step, shares)
    block = order[2 * ctx + e]
    slot = (block >= blocks // 2).astype(jnp.int32)
    queries = iq[...].reshape(share * heads, dim)
    weights = jnp.broadcast_to(
        scaled[pl.ds(pl.multiple_of(step * share, share), share), :][:, :, None], (share, heads, 128)
    )
    query_grad[...] = jnp.zeros_like(query_grad)

    def grad_tile(k, carry):
        cols = pl.ds(pl.multiple_of(k * tile, tile), tile)
        keys = idx[cols, :]
        dots = lax.dot_general(
            queries, keys, NT_DIMS, preferred_element_type=jnp.float32
        ).reshape(share, heads, tile)
        rate = grad[part, slot, :, cols].astype(jnp.float32)
        parts = [
            jnp.where(
                dots[:, :, c : c + 128] > 0, rate[:, None, c : c + 128] * weights, 0.0
            )
            for c in range(0, tile, 128)
        ]
        coefficient = (
            jnp.concatenate(parts, axis=2).reshape(share * heads, tile).astype(jnp.bfloat16)
        )
        query_grad[...] += jnp.dot(
            coefficient, keys, preferred_element_type=jnp.float32
        ).reshape(share, heads, dim)
        total[cols, :] += lax.dot_general(
            coefficient, queries, TN_DIMS, preferred_element_type=jnp.float32
        )
        return carry

    lax.fori_loop(0, (block * half + half - 1) // tile + 1, grad_tile, 0)

    @pl.when(step == steps - 1)
    def _():
        def store(r, carry):
            dst = pl.ds(pl.multiple_of(r * half, half), half)
            src = pl.ds(pl.multiple_of(order[r] * half, half), half)
            key_grad[dst, :] = total[src, :]
            return carry

        lax.fori_loop(0, blocks, store, 0)


def backward(order, iq, iw, grad, idx, shares):
    rows, heads, dim = iq.shape
    share = rows // 2 // shares
    tile = 256
    return pl.pallas_call(
        functools.partial(backward_kernel, shares, tile),
        out_shape=(
            jax.ShapeDtypeStruct(iq.shape, jnp.float32),
            jax.ShapeDtypeStruct(idx.shape, jnp.float32),
        ),
        grid_spec=pltpu.PrefetchScalarGridSpec(
            num_scalar_prefetch=1,
            grid=(2 * shares,),
            in_specs=[
                pl.BlockSpec((share, heads, dim), lambda i, o: (i, 0, 0)),
                pl.BlockSpec(iw.shape, lambda i, o: (0, 0)),
                pl.BlockSpec(grad.shape, lambda i, o: (0, 0, 0, 0)),
                pl.BlockSpec(idx.shape, lambda i, o: (0, 0)),
            ],
            out_specs=[
                pl.BlockSpec((share, heads, dim), lambda i, o: (i, 0, 0)),
                pl.BlockSpec(idx.shape, lambda i, o: (0, 0)),
            ],
            scratch_shapes=[
                pltpu.VMEM(idx.shape, jnp.float32), pltpu.VMEM((rows, heads), jnp.float32)
            ],
        ),
        name="backward",
    )(order, iq, iw, grad, idx)


def reduce_kernel(groups, shares, parts, out, near, mid, far, acc, last, ns, nr, ms, mr, fs, fr):
    ctx, head = lax.axis_index("ctx"), lax.axis_index("head")
    group, core = ctx // 2, lax.rem(ctx, 2)
    sibling = group * 2 + 1 - core
    rows = out.shape[0]
    enter(groups, shares)
    sent = []
    for step in [*range(1, groups), 0]:
        peer = lax.rem(group + step, groups)
        copy = remote(
            parts.at[peer * 2 + 1 - core], near.at[step], ns.at[step], nr.at[step], {"ctx": sibling}
        )
        copy.start()
        sent.append(copy)
    for step in range(1, groups):
        peer = lax.rem(group + step, groups)
        remote(near.at[step], near.at[step], ns.at[step], nr.at[step], {"ctx": sibling}).wait_recv()
        acc[step] = parts[peer * 2 + core] + near[step]
        copy = remote(
            acc.at[step], mid.at[step], ms.at[step], mr.at[step], {"ctx": peer * 2 + core}
        )
        copy.start()
        sent.append(copy)
    remote(near.at[0], near.at[0], ns.at[0], nr.at[0], {"ctx": sibling}).wait_recv()
    value = parts[ctx] + near[0]
    for step in range(1, groups):
        remote(mid.at[step], mid.at[step], ms.at[step], mr.at[step], {"ctx": sibling}).wait_recv()
        value = value + mid[step]
    last[...] = value
    for step in range(1, shares):
        peer = lax.rem(head + step, shares)
        copy = remote(
            last.at[pl.ds(pl.multiple_of(peer * rows, rows), rows)], far.at[step], fs.at[step],
            fr.at[step], {"head": peer},
        )
        copy.start()
        sent.append(copy)
    value = last[pl.ds(pl.multiple_of(head * rows, rows), rows), :]
    for step in range(1, shares):
        remote(far.at[step], far.at[step], fs.at[step], fr.at[step], {"head": head}).wait_recv()
        value = value + far[step]
    out[...] = value
    for copy in sent:
        copy.wait_send()


def reduce(parts, cycle, shares):
    groups = cycle // 2
    rows, dim = parts.shape[0] // cycle, parts.shape[1]
    dma = pltpu.SemaphoreType.DMA
    buffer = pltpu.VMEM((groups, rows, dim), jnp.float32)
    return pl.pallas_call(
        functools.partial(reduce_kernel, groups, shares),
        out_shape=jax.ShapeDtypeStruct((rows // shares, dim), jnp.float32),
        in_specs=[pl.BlockSpec(memory_space=pltpu.VMEM)],
        out_specs=pl.BlockSpec(memory_space=pltpu.VMEM),
        scratch_shapes=[
            buffer, buffer, pltpu.VMEM((shares, rows // shares, dim), jnp.float32), buffer,
            pltpu.VMEM((rows, dim), jnp.float32),
            dma((groups,)), dma((groups,)), dma((groups,)), dma((groups,)),
            dma((shares,)), dma((shares,)),
        ],
        compiler_params=pltpu.CompilerParams(collective_id=2, has_side_effects=True),
        name="reduce",
    )(parts.reshape(cycle, rows, dim))


def per_device(
    block_order, query_latent, key_latent, normalizer, indexer_query, indexer_key, indexer_weight
):
    cycle, shares = lax.axis_size("ctx"), lax.axis_size("head")
    weight = indexer_weight.T
    partial, idx, iq, iw = gather(
        key_latent.T, indexer_key, indexer_query, weight, query_latent.transpose(1, 2, 0),
        normalizer.T, cycle, shares,
    )
    idx = idx.reshape(-1, idx.shape[2])
    sums, probs, idx_sorted = forward(
        block_order, partial.reshape(-1, partial.shape[2]), idx, iq, iw, shares
    )
    grad = gradient(sums, probs, shares)
    query_grad, key_parts = backward(
        block_order, indexer_query, weight, grad, idx_sorted, shares
    )
    return query_grad, reduce(key_parts, cycle, shares)


def solution(mesh):
    return jax.shard_map(
        per_device,
        mesh=mesh,
        in_specs=(
            P(),
            P("ctx", "head", None),
            P("ctx", None),
            P("ctx", "head"),
            P("ctx", "head", None),
            P("ctx", None),
            P("ctx", "head"),
        ),
        out_specs=(P("ctx", "head", None), P(("ctx", "head"), None)),
        check_vma=False,
    )
```

```python
import functools
import math

import jax
import jax.numpy as jnp
from jax import lax
from jax.experimental import pallas as pl
from jax.experimental.pallas import tpu as pltpu
from jax.sharding import PartitionSpec as P

MESH = pl.DeviceIdType.MESH
mla_scale = 192.0 ** (-0.5)
loss_scale = 64.0
log2e = math.log2(math.e)
NT_DIMS = (((1,), (1,)), ((), ()))
TN_DIMS = (((0,), (0,)), ((), ()))


def enter(groups, shares):
    ctx, head = lax.axis_index("ctx"), lax.axis_index("head")
    group, core = ctx // 2, lax.rem(ctx, 2)
    barrier = pltpu.get_barrier_semaphore()
    count = 0
    if groups:
        for step in range(1, groups):
            peer = lax.rem(group + step, groups) * 2 + core
            pl.semaphore_signal(barrier, 1, device_id={"ctx": peer}, device_id_type=MESH)
        pl.semaphore_signal(
            barrier, 1, device_id={"ctx": group * 2 + 1 - core}, device_id_type=MESH
        )
        count += groups
    for step in range(1, shares):
        peer = lax.rem(head + step, shares)
        pl.semaphore_signal(barrier, 1, device_id={"head": peer}, device_id_type=MESH)
    count += shares - 1
    pl.semaphore_wait(barrier, count)


def remote(src, dst, send, recv, device):
    return pltpu.make_async_remote_copy(
        src_ref=src, dst_ref=dst, send_sem=send, recv_sem=recv, device_id=device, device_id_type=MESH
    )


def partner(group, step, groups):
    bit = 1
    while bit < groups:
        if step & bit:
            group = group + bit * (1 - 2 * lax.rem(group // bit, 2))
        bit *= 2
    return group


def gather_kernel(
    groups, shares, lat, idx, iq, iw, q_far, norm, acc, all_idx, iq_recv, iw_recv,
    all_lat, q, keys, local, qs, qr, ws, wr, ds, dr, fs, fr,
):
    ctx, head = lax.axis_index("ctx"), lax.axis_index("head")
    group, core = ctx // 2, lax.rem(ctx, 2)
    sibling = group * 2 + 1 - core
    rows = idx.shape[0]
    half = rows // 2
    share = half // shares
    own = [
        pltpu.make_async_copy(lat, all_lat.at[ctx], local.at[0]),
        pltpu.make_async_copy(idx, all_idx.at[ctx], local.at[1]),
    ]
    for e in range(2):
        take = pl.ds(pl.multiple_of(e * half + head * share, share), share)
        own.append(pltpu.make_async_copy(iq.at[take], iq_recv.at[head, e], local.at[2 + e]))
    own.append(pltpu.make_async_copy(iw, iw_recv.at[head], local.at[4]))
    own.append(pltpu.make_async_copy(q_far, q, local.at[5]))
    for copy in own:
        copy.start()
    heads, bundle = q.shape[0], 8

    def score(source):
        keys[...] = jnp.concatenate((all_lat[2 * source], all_lat[2 * source + 1]), axis=1).T

        def body(i, total):
            shift = norm[pl.ds(pl.multiple_of(i * bundle, bundle), bundle), :] * log2e
            for h in range(0, bundle, 2):
                pair = jnp.concatenate((q[i * bundle + h], q[i * bundle + h + 1]), axis=1)
                scores = jnp.dot(keys[...], pair, preferred_element_type=jnp.float32) * (
                    mla_scale * log2e
                )
                total = total + jnp.exp2(scores[:, :rows] - shift[h : h + 1])
                total = total + jnp.exp2(scores[:, rows:] - shift[h + 1 : h + 2])
            return total

        acc[source] = lax.fori_loop(
            0, heads // bundle, body, jnp.zeros((2 * rows, rows), jnp.float32)
        )

    enter(groups, shares)
    sent = []
    for step in range(1, groups):
        peer = partner(group, step, groups) * 2 + core
        for k, (src, dst) in enumerate(((lat, all_lat), (idx, all_idx))):
            copy = remote(src, dst.at[ctx], ds.at[k, step], dr.at[k, step], {"ctx": peer})
            copy.start()
            sent.append(copy)
    for k, (src, dst) in enumerate(((lat, all_lat), (idx, all_idx))):
        copy = remote(src, dst.at[ctx], fs.at[k, 0], fr.at[k, 0], {"ctx": sibling})
        copy.start()
        sent.append(copy)
    for step in range(1, shares):
        peer = lax.rem(head + step, shares)
        for e in range(2):
            take = pl.ds(pl.multiple_of(e * half + peer * share, share), share)
            copy = remote(
                iq.at[take], iq_recv.at[head, e], qs.at[step, e], qr.at[step, e], {"head": peer}
            )
            copy.start()
            sent.append(copy)
        copy = remote(iw, iw_recv.at[head], ws.at[step], wr.at[step], {"head": peer})
        copy.start()
        sent.append(copy)
    slot = all_lat.at[sibling]
    remote(slot, slot, fs.at[0, 0], fr.at[0, 0], {"ctx": sibling}).wait_recv()
    own[0].wait()
    own[-1].wait()
    score(group)
    slot = all_idx.at[sibling]
    remote(slot, slot, fs.at[1, 0], fr.at[1, 0], {"ctx": sibling}).wait_recv()

    def relay(step):
        source = partner(group, step, groups) * 2 + core
        for k, dst in enumerate((all_lat, all_idx)):
            slot = dst.at[source]
            remote(slot, slot, ds.at[k, step], dr.at[k, step], {"ctx": sibling}).wait_recv()
            copy = remote(slot, slot, fs.at[k, step], fr.at[k, step], {"ctx": sibling})
            copy.start()
            sent.append(copy)

    def consume(step):
        source = partner(group, step, groups)
        for k, dst in enumerate((all_lat, all_idx)):
            slot = dst.at[source * 2 + 1 - core]
            remote(slot, slot, fs.at[k, step], fr.at[k, step], {"ctx": sibling}).wait_recv()
        score(source)

    for step in range(1, groups + 1):
        if step < groups:
            relay(step)
        if 0 < step - 1 < groups:
            consume(step - 1)
    for step in range(1, shares):
        source = lax.rem(head + shares - step, shares)
        for e in range(2):
            slot = iq_recv.at[source, e]
            remote(slot, slot, qs.at[step, e], qr.at[step, e], {"head": source}).wait_recv()
        slot = iw_recv.at[source]
        remote(slot, slot, ws.at[step], wr.at[step], {"head": source}).wait_recv()
    for copy in sent:
        copy.wait_send()
    for copy in own[1:-1]:
        copy.wait()


def gather(lat, idx, iq, iw, q, norm, cycle, shares):
    groups = cycle // 2
    rows = idx.shape[0]
    share = rows // 2 // shares
    dma = pltpu.SemaphoreType.DMA
    return pl.pallas_call(
        functools.partial(gather_kernel, groups, shares),
        out_shape=(
            jax.ShapeDtypeStruct((groups, 2 * rows, rows), jnp.float32),
            jax.ShapeDtypeStruct((cycle,) + idx.shape, idx.dtype),
            jax.ShapeDtypeStruct((shares, 2, share) + iq.shape[1:], iq.dtype),
            jax.ShapeDtypeStruct((shares,) + iw.shape, iw.dtype),
        ),
        in_specs=[pl.BlockSpec(memory_space=pl.ANY)] * 5
        + [pl.BlockSpec(memory_space=pltpu.VMEM)],
        out_specs=[pl.BlockSpec(memory_space=pltpu.VMEM)] * 4,
        scratch_shapes=[
            pltpu.VMEM((cycle,) + lat.shape, lat.dtype),
            pltpu.VMEM(q.shape, q.dtype),
            pltpu.VMEM((2 * rows, lat.shape[0]), lat.dtype),
            dma((6,)),
            dma((shares, 2)), dma((shares, 2)), dma((shares,)), dma((shares,)),
            dma((2, groups)), dma((2, groups)), dma((2, groups)), dma((2, groups)),
        ],
        compiler_params=pltpu.CompilerParams(collective_id=0, has_side_effects=True),
        name="gather",
    )(lat, idx, iq, iw, q, norm)


def forward_kernel(
    shares, tile, order, lat, idx, iq, iw, sums, probs, idx_sorted, logits, acc
):
    ctx, head = lax.axis_index("ctx"), lax.axis_index("head")
    blocks = order.shape[0]
    tokens = idx.shape[0]
    half = tokens // blocks
    rows = 2 * half
    tiles = tokens // tile
    share = half // shares
    idx_heads = iq.shape[3]
    idx_scale = (idx_heads * shares * iq.shape[4]) ** (-0.5)

    def sort(c, carry):
        for e in range(2):
            src = pl.ds(pl.multiple_of((2 * c + e) * half, half), half)
            dst = pl.ds(pl.multiple_of(order[2 * c + e] * half, half), half)
            acc[dst, :] = lat[src, :]
            idx_sorted[dst, :] = idx[src, :]
        return carry

    lax.fori_loop(0, blocks // 2, sort, 0)
    for e in range(2):
        block = order[2 * ctx + e]
        slot = (block >= blocks // 2).astype(jnp.int32)
        first = block * half + head * share
        logits[...] = jnp.full(logits.shape, -jnp.inf, jnp.float32)
        weights = []
        for z in range(shares):
            flat = iw[z].astype(jnp.float32).T * idx_scale
            flat = sum(
                jnp.where(head == y, flat[e * half + y * share : e * half + (y + 1) * share], 0.0)
                for y in range(shares)
            )
            weights.append(jnp.broadcast_to(flat[:, :, None], (share, idx_heads, 128)))

        def logit_tile(k, carry):
            cols = pl.ds(pl.multiple_of(k * tile, tile), tile)
            keys = idx_sorted[cols, :]
            total = jnp.zeros((share, tile), jnp.float32)
            for z in range(shares):
                dots = lax.dot_general(
                    iq[z, e].reshape(share * idx_heads, -1), keys, NT_DIMS,
                    preferred_element_type=jnp.float32,
                ).reshape(share, idx_heads, tile)
                parts = [
                    jnp.sum(weights[z] * jnp.maximum(dots[:, :, c : c + 128], 0.0), axis=1)
                    for c in range(0, tile, 128)
                ]
                total = total + jnp.concatenate(parts, axis=1)
            shape = (share, tile)
            visible = k * tile + lax.broadcasted_iota(
                jnp.int32, shape, 1
            ) <= first + lax.broadcasted_iota(jnp.int32, shape, 0)
            logits[:, cols] = jnp.where(visible, total, -jnp.inf)
            return carry

        lax.fori_loop(0, (block * half + half - 1) // tile + 1, logit_tile, 0)
        values = logits[...]
        top = jnp.max(values, axis=1, keepdims=True)
        expo = jnp.exp(values - top)
        norm_sum = jnp.sum(expo, axis=1, keepdims=True)
        probs[pl.ds(pl.multiple_of(slot * share, share), share), :] = expo / norm_sum

    def finish(k, carry):
        cols = pl.ds(pl.multiple_of(k * tile, tile), tile)
        total = acc[cols, :].T
        shape = (half, tile)
        for e in range(2):
            block = order[2 * ctx + e]
            slot = (block >= blocks // 2).astype(jnp.int32)
            visible = k * tile + lax.broadcasted_iota(
                jnp.int32, shape, 1
            ) <= block * half + lax.broadcasted_iota(jnp.int32, shape, 0)
            sums[pl.ds(pl.multiple_of(slot * half, half), half), cols] = jnp.where(
                visible, total[e * half : (e + 1) * half], 0.0
            )
        return carry

    lax.fori_loop(0, tiles, finish, 0)


def forward(order, lat, idx, iq, iw, shares):
    tokens, rows = lat.shape
    share = rows // 2 // shares
    vmem = pl.BlockSpec(memory_space=pltpu.VMEM)
    return pl.pallas_call(
        functools.partial(forward_kernel, shares, math.gcd(tokens // 2, 512)),
        out_shape=(
            jax.ShapeDtypeStruct((rows, tokens), jnp.float32),
            jax.ShapeDtypeStruct((2 * share, tokens), jnp.float32),
            jax.ShapeDtypeStruct(idx.shape, idx.dtype),
        ),
        in_specs=[pl.BlockSpec(memory_space=pltpu.SMEM)] + [vmem] * 4,
        out_specs=[vmem] * 3,
        scratch_shapes=[
            pltpu.VMEM((share, tokens), jnp.float32),
            pltpu.VMEM((tokens, rows), jnp.float32),
        ],
        name="forward",
    )(order, lat, idx, iq, iw)


def gradient_kernel(shares, sums, probs, grad, short_sums, low, high, ls, lr, hs, hr, gs, gr):
    head = lax.axis_index("head")
    rows, tokens = sums.shape
    half = rows // 2
    share = half // shares
    short = tokens // 2
    short_sums[...] = sums[...].astype(jnp.bfloat16)
    enter(0, shares)
    sent = []
    for step in range(1, shares):
        peer = lax.rem(head + step, shares)
        start = pl.multiple_of(peer * share, share)
        for copy in (
            remote(
                short_sums.at[pl.ds(start, share), pl.ds(0, short)], low.at[step], ls.at[step],
                lr.at[step], {"head": peer},
            ),
            remote(
                short_sums.at[pl.ds(half + start, share)], high.at[step], hs.at[step], hr.at[step],
                {"head": peer},
            ),
        ):
            copy.start()
            sent.append(copy)
    start = pl.multiple_of(head * share, share)
    total_low = sums[pl.ds(start, share), :short]
    total_high = sums[pl.ds(half + start, share), :]
    for step in range(1, shares):
        source = lax.rem(head + shares - step, shares)
        remote(low.at[step], low.at[step], ls.at[step], lr.at[step], {"head": source}).wait_recv()
        total_low = total_low + low[step].astype(jnp.float32)
        remote(high.at[step], high.at[step], hs.at[step], hr.at[step], {"head": source}).wait_recv()
        total_high = total_high + high[step].astype(jnp.float32)
    row_low = jnp.sum(total_low, axis=1, keepdims=True)
    row_high = jnp.sum(total_high, axis=1, keepdims=True)
    grad[head, 0, :, :short] = (
        loss_scale * (probs[:share, :short] - total_low / row_low)
    ).astype(jnp.bfloat16)
    grad[head, 1] = (loss_scale * (probs[share:, :] - total_high / row_high)).astype(jnp.bfloat16)
    for step in range(1, shares):
        peer = lax.rem(head + step, shares)
        for copy in (
            remote(
                grad.at[head, 0, :, pl.ds(0, short)], grad.at[head, 0, :, pl.ds(0, short)],
                gs.at[0, step], gr.at[0, step], {"head": peer},
            ),
            remote(
                grad.at[head, 1], grad.at[head, 1], gs.at[1, step], gr.at[1, step], {"head": peer}
            ),
        ):
            copy.start()
            sent.append(copy)
    for step in range(1, shares):
        source = lax.rem(head + shares - step, shares)
        slot = grad.at[source, 0, :, pl.ds(0, short)]
        remote(slot, slot, gs.at[0, step], gr.at[0, step], {"head": source}).wait_recv()
        slot = grad.at[source, 1]
        remote(slot, slot, gs.at[1, step], gr.at[1, step], {"head": source}).wait_recv()
    for copy in sent:
        copy.wait_send()


def gradient(sums, probs, shares):
    rows, tokens = sums.shape
    share = rows // 2 // shares
    dma = pltpu.SemaphoreType.DMA
    return pl.pallas_call(
        functools.partial(gradient_kernel, shares),
        out_shape=jax.ShapeDtypeStruct((shares, 2, share, tokens), jnp.bfloat16),
        in_specs=[pl.BlockSpec(memory_space=pltpu.VMEM)] * 2,
        out_specs=pl.BlockSpec(memory_space=pltpu.VMEM),
        scratch_shapes=[
            pltpu.VMEM(sums.shape, jnp.bfloat16),
            pltpu.VMEM((shares, share, tokens // 2), jnp.bfloat16),
            pltpu.VMEM((shares, share, tokens), jnp.bfloat16),
            dma((shares,)), dma((shares,)), dma((shares,)), dma((shares,)),
            dma((2, shares)), dma((2, shares)),
        ],
        compiler_params=pltpu.CompilerParams(collective_id=1, has_side_effects=True),
        name="gradient",
    )(sums, probs)


def backward_kernel(shares, tile, order, iq, iw, grad, idx, query_grad, key_grad, total, scaled):
    step, steps = pl.program_id(0), pl.num_programs(0)
    ctx = lax.axis_index("ctx")
    blocks = order.shape[0]
    tokens = idx.shape[0]
    half = tokens // blocks
    count, heads, dim = iq.shape
    share = grad.shape[2]
    parts_each = count // share
    idx_scale = (heads * shares * dim) ** (-0.5)

    @pl.when(step == 0)
    def _():
        total[...] = jnp.zeros_like(total)
        scaled[...] = iw[...].astype(jnp.float32).T * idx_scale

    e = step // (steps // 2)
    part = pl.ds(lax.rem(step, steps // 2) * parts_each, parts_each)
    block = order[2 * ctx + e]
    slot = (block >= blocks // 2).astype(jnp.int32)
    queries = iq[...].reshape(count * heads, dim)
    weights = jnp.broadcast_to(
        scaled[pl.ds(pl.multiple_of(step * count, count), count), :][:, :, None], (count, heads, 128)
    )
    query_grad[...] = jnp.zeros_like(query_grad)

    def grad_tile(k, carry):
        cols = pl.ds(pl.multiple_of(k * tile, tile), tile)
        keys = idx[cols, :]
        dots = lax.dot_general(
            queries, keys, NT_DIMS, preferred_element_type=jnp.float32
        ).reshape(count, heads, tile)
        rate = grad[part, slot, :, cols].reshape(count, tile).astype(jnp.float32)
        parts = [
            jnp.where(
                dots[:, :, c : c + 128] > 0, rate[:, None, c : c + 128] * weights, 0.0
            )
            for c in range(0, tile, 128)
        ]
        coefficient = (
            jnp.concatenate(parts, axis=2).reshape(count * heads, tile).astype(jnp.bfloat16)
        )
        query_grad[...] += jnp.dot(
            coefficient, keys, preferred_element_type=jnp.float32
        ).reshape(count, heads, dim)
        total[cols, :] += lax.dot_general(
            coefficient, queries, TN_DIMS, preferred_element_type=jnp.float32
        )
        return carry

    lax.fori_loop(0, (block * half + half - 1) // tile + 1, grad_tile, 0)

    @pl.when(step == steps - 1)
    def _():
        def store(r, carry):
            dst = pl.ds(pl.multiple_of(r * half, half), half)
            src = pl.ds(pl.multiple_of(order[r] * half, half), half)
            key_grad[dst, :] = total[src, :]
            return carry

        lax.fori_loop(0, blocks, store, 0)


def backward(order, iq, iw, grad, idx, shares):
    rows, heads, dim = iq.shape
    share = rows // 2 // shares
    count = share * shares
    tile = math.gcd(idx.shape[0] // 2, 512)
    return pl.pallas_call(
        functools.partial(backward_kernel, shares, tile),
        out_shape=(
            jax.ShapeDtypeStruct(iq.shape, jnp.float32),
            jax.ShapeDtypeStruct(idx.shape, jnp.float32),
        ),
        grid_spec=pltpu.PrefetchScalarGridSpec(
            num_scalar_prefetch=1,
            grid=(rows // count,),
            in_specs=[
                pl.BlockSpec((count, heads, dim), lambda i, o: (i, 0, 0)),
                pl.BlockSpec(iw.shape, lambda i, o: (0, 0)),
                pl.BlockSpec(grad.shape, lambda i, o: (0, 0, 0, 0)),
                pl.BlockSpec(idx.shape, lambda i, o: (0, 0)),
            ],
            out_specs=[
                pl.BlockSpec((count, heads, dim), lambda i, o: (i, 0, 0)),
                pl.BlockSpec(idx.shape, lambda i, o: (0, 0)),
            ],
            scratch_shapes=[
                pltpu.VMEM(idx.shape, jnp.float32), pltpu.VMEM((rows, heads), jnp.float32)
            ],
        ),
        name="backward",
    )(order, iq, iw, grad, idx)


def reduce_kernel(groups, shares, parts, out, near, mid, far, acc, last, ns, nr, ms, mr, fs, fr):
    ctx, head = lax.axis_index("ctx"), lax.axis_index("head")
    group, core = ctx // 2, lax.rem(ctx, 2)
    sibling = group * 2 + 1 - core
    rows = out.shape[0]
    enter(groups, shares)
    sent = []
    for step in [*range(1, groups), 0]:
        peer = lax.rem(group + step, groups)
        copy = remote(
            parts.at[peer * 2 + 1 - core], near.at[step], ns.at[step], nr.at[step], {"ctx": sibling}
        )
        copy.start()
        sent.append(copy)
    for step in range(1, groups):
        peer = lax.rem(group + step, groups)
        remote(near.at[step], near.at[step], ns.at[step], nr.at[step], {"ctx": sibling}).wait_recv()
        acc[step] = (parts[peer * 2 + core] + near[step]).astype(jnp.bfloat16)
        copy = remote(
            acc.at[step], mid.at[step], ms.at[step], mr.at[step], {"ctx": peer * 2 + core}
        )
        copy.start()
        sent.append(copy)
    remote(near.at[0], near.at[0], ns.at[0], nr.at[0], {"ctx": sibling}).wait_recv()
    value = parts[ctx] + near[0]
    for step in range(1, groups):
        remote(mid.at[step], mid.at[step], ms.at[step], mr.at[step], {"ctx": sibling}).wait_recv()
        value = value + mid[step].astype(jnp.float32)
    last[...] = value
    for step in range(1, shares):
        peer = lax.rem(head + step, shares)
        copy = remote(
            last.at[pl.ds(pl.multiple_of(peer * rows, rows), rows)], far.at[step], fs.at[step],
            fr.at[step], {"head": peer},
        )
        copy.start()
        sent.append(copy)
    value = last[pl.ds(pl.multiple_of(head * rows, rows), rows), :]
    for step in range(1, shares):
        remote(far.at[step], far.at[step], fs.at[step], fr.at[step], {"head": head}).wait_recv()
        value = value + far[step]
    out[...] = value
    for copy in sent:
        copy.wait_send()


def reduce(parts, cycle, shares):
    groups = cycle // 2
    rows, dim = parts.shape[0] // cycle, parts.shape[1]
    dma = pltpu.SemaphoreType.DMA
    buffer = pltpu.VMEM((groups, rows, dim), jnp.bfloat16)
    return pl.pallas_call(
        functools.partial(reduce_kernel, groups, shares),
        out_shape=jax.ShapeDtypeStruct((rows // shares, dim), jnp.float32),
        in_specs=[pl.BlockSpec(memory_space=pltpu.VMEM)],
        out_specs=pl.BlockSpec(memory_space=pltpu.VMEM),
        scratch_shapes=[
            pltpu.VMEM((groups, rows, dim), jnp.float32), buffer,
            pltpu.VMEM((shares, rows // shares, dim), jnp.float32), buffer,
            pltpu.VMEM((rows, dim), jnp.float32),
            dma((groups,)), dma((groups,)), dma((groups,)), dma((groups,)),
            dma((shares,)), dma((shares,)),
        ],
        compiler_params=pltpu.CompilerParams(collective_id=2, has_side_effects=True),
        name="reduce",
    )(parts.reshape(cycle, rows, dim))


def per_device(
    block_order, query_latent, key_latent, normalizer, indexer_query, indexer_key, indexer_weight
):
    cycle, shares = lax.axis_size("ctx"), lax.axis_size("head")
    weight = indexer_weight.T
    partial, idx, iq, iw = gather(
        key_latent.T, indexer_key, indexer_query, weight, query_latent.transpose(1, 2, 0),
        normalizer.T, cycle, shares,
    )
    idx = idx.reshape(-1, idx.shape[2])
    sums, probs, idx_sorted = forward(
        block_order, partial.reshape(-1, partial.shape[2]), idx, iq, iw, shares
    )
    grad = gradient(sums, probs, shares)
    query_grad, key_parts = backward(
        block_order, indexer_query, weight, grad, idx_sorted, shares
    )
    return query_grad, reduce(key_parts, cycle, shares)


def solution(mesh):
    return jax.shard_map(
        per_device,
        mesh=mesh,
        in_specs=(
            P(),
            P("ctx", "head", None),
            P("ctx", None),
            P("ctx", "head"),
            P("ctx", "head", None),
            P("ctx", None),
            P("ctx", "head"),
        ),
        out_specs=(P("ctx", "head", None), P(("ctx", "head"), None)),
        check_vma=False,
    )
```
